32 devices in a mesh: dp: 8 (over z, x), tensor: 4 (over y, core).
Axes of the slice: x: 2, y: 2, z: 4, core: 2. Of those that a mesh axis runs over, the one named last changes fastest.
Arguments:
- clip_tokens: bfloat16 [8, 1568, 768], P('dp', 'tensor'), as said below
- time_qkv: bfloat16 [3, 768, 768], P(None, 'dp', 'tensor'), may hold values from -0.21875 to 0.21875
- time_out: bfloat16 [768, 768], P('tensor', 'dp'), may hold values from -0.625 to 0.625
- time_mixer: bfloat16 [768, 768], P(('dp', 'tensor')), may hold values from -0.21875 to 0.21875
- space_qkv: bfloat16 [3, 768, 768], P(None, 'dp', 'tensor'), may hold values from -0.21875 to 0.21875
- space_out: bfloat16 [768, 768], P('tensor', 'dp'), may hold values from -3.5 to 3.5
- hidden_in: bfloat16 [768, 3072], P('dp', 'tensor'), may hold values from -0.21875 to 0.21875
- hidden_out: bfloat16 [3072, 768], P('tensor', 'dp'), may hold values from -0.109375 to 0.109375
- norm_gain: bfloat16 [3, 768], P(None, ('dp', 'tensor')), may hold values from 0.25 to 1.75
- norm_bias: bfloat16 [3, 768], P(None, ('dp', 'tensor')), may hold values from -3 to 3
- cotangent: bfloat16 [8, 1568, 768], P('dp', 'tensor'), may hold values from -6 to 6
Outputs:
- block_out: float32 [8, 1568, 768], P('dp', 'tensor')
- input_grad: float32 [8, 1568, 768], P('dp', 'tensor')
- time_qkv_grad: float32 [3, 768, 768], P(None, 'dp', 'tensor')
- time_out_grad: float32 [768, 768], P('tensor', 'dp')
- time_mixer_grad: float32 [768, 768], P(('dp', 'tensor'))
- space_qkv_grad: float32 [3, 768, 768], P(None, 'dp', 'tensor')
- space_out_grad: float32 [768, 768], P('tensor', 'dp')
- hidden_in_grad: float32 [768, 3072], P('dp', 'tensor')
- hidden_out_grad: float32 [3072, 768], P('tensor', 'dp')
- gain_grad: float32 [3, 768], P(None, ('dp', 'tensor'))
- bias_grad: float32 [3, 768], P(None, ('dp', 'tensor'))
- qk_clip: float32 [2, 12], P(None, 'tensor')
The draws below stay inside these ranges and needn't reach their ends.
Inputs may be any that keep to these rules, and one draw needn't show every extreme that they name: `clip_tokens`: 8 clips of tokens of order one.
All inputs are finite; a program needn't handle non-finite values.
Results may differ from the reference program's by a relative error of at most 0.035.
Values may be sent and summed in bfloat16 or wider, within the bound.
No kernel may reach another device: no remote copies, remote signals or barrier semaphores. Data moves between devices by JAX's collectives and lax.ppermute only.
A program may use at most 128 MiB of HBM per device.

```python
import jax
import jax.numpy as jnp
from jax import lax

D = 768
HD = 64
FF = 3072
FRAMES = 8
PATCHES = 196
CLIPS = 8
N_TENSOR = 4


def draw_clip_tokens(key, part):
    noise_key, line_key = jax.random.split(key)
    full_shape = (CLIPS, FRAMES * PATCHES, D)
    noise = jax.random.normal(noise_key, full_shape, jnp.float32)
    height = 2.0
    direction = jnp.clip(jax.random.normal(line_key, (D,), jnp.float32), -3.0, 3.0)
    ramp = height * jnp.arange(CLIPS, dtype=jnp.float32) / (CLIPS - 1)
    return (noise + ramp[:, None, None] * direction[None, None, :]).astype(jnp.bfloat16)


def block_scale(stream_key, shape, pieces, smallest, top_value):
    level = 1.0
    for axis_at, shards_of in pieces:
        heights = jax.random.uniform(jax.random.fold_in(jax.random.fold_in(stream_key, 6), axis_at), (shards_of,), jnp.float32, smallest / len(pieces), top_value / len(pieces))
        level = level * jnp.repeat(jnp.exp(heights), shape[axis_at] // shards_of).reshape((-1,) + (1,) * (len(shape) - 1 - axis_at))
    return level


def scatter_about(stream_key, shape, deviation, limit, cuts=(), held_as=jnp.bfloat16):
    loudness = block_scale(stream_key, shape, cuts, -0.22, 0.18) if cuts else 1.0
    values = jax.random.normal(stream_key, shape, jnp.float32) * deviation * loudness
    return jnp.minimum(jnp.maximum(values, -limit), limit).astype(held_as)


def setup_inputs(seed: int = 0) -> dict:
    arg_keys = jax.random.split(jax.random.key(seed), 12)
    return {
        "clip_tokens": draw_clip_tokens(jax.random.fold_in(arg_keys[11], 71), 0),
        "time_qkv": scatter_about(arg_keys[1], (3, D, D), D ** -0.5, 0.21875, ((1, 8), (2, 4))),
        "time_out": scatter_about(arg_keys[2], (D, D), (D // FRAMES) ** -0.5, 0.625, ((0, 4), (1, 8))),
        "time_mixer": scatter_about(arg_keys[3], (D, D), D ** -0.5, 0.21875, ((0, 32),)),
        "space_qkv": scatter_about(arg_keys[4], (3, D, D), D ** -0.5, 0.21875, ((1, 8), (2, 4))),
        "space_out": scatter_about(arg_keys[5], (D, D), (D // PATCHES) ** -0.5, 3.5, ((0, 4), (1, 8))),
        "hidden_in": scatter_about(arg_keys[6], (D, FF), D ** -0.5, 0.21875, ((0, 8), (1, 4))),
        "hidden_out": scatter_about(arg_keys[7], (FF, D), FF ** -0.5, 0.109375, ((0, 4), (1, 8))),
        "norm_gain": jnp.clip(1.0 + 0.15 * jax.random.normal(arg_keys[8], (3, D), jnp.float32), 0.25, 1.75).astype(jnp.bfloat16),
        "norm_bias": scatter_about(arg_keys[9], (3, D), 0.5, 3.0, ((1, 32),)),
        "cotangent": scatter_about(arg_keys[10], (CLIPS, FRAMES * PATCHES, D), 1.0, 6.0, ((0, 8), (1, 4))),
    }


SCALE = 0.125
TAU = 2.0
EPS = 1e-06
TIME_FORMS = ('cfphe,cgphe->cphfg', 'cphfg,cgphe->cfphe')
SPACE_FORMS = ('cfphe,cfqhe->cfhpq', 'cfhpq,cfqhe->cfphe')

@jax.custom_vjp
def low(v):
    return lax.optimization_barrier(v.astype(jnp.bfloat16)).astype(jnp.float32)

@jax.custom_vjp
def low_back(v):
    return v

def low_keep(v):
    return (low(v), None)

def low_pass(kept, grad):
    return (grad,)

def back_keep(v):
    return (v, None)

def back_low(kept, grad):
    return (low(grad),)
low.defvjp(low_keep, low_pass)
low_back.defvjp(back_keep, back_low)

def product(form, left, right):
    return jnp.einsum(form, left, right, precision=lax.Precision.HIGHEST)

def normalize(row_block, gain_row, bias_row):
    row_mean = lax.optimization_barrier(jnp.mean(row_block, axis=-1, keepdims=True))
    centered = row_block - row_mean
    variance = lax.optimization_barrier(jnp.mean(centered * centered, axis=-1, keepdims=True))
    return centered * lax.rsqrt(variance + EPS) * gain_row + bias_row

def attention(hidden, weight_qkv, weight_out, forms):
    clip_count, seq_len, width = hidden.shape
    group_width = width // N_TENSOR
    heads_loc = group_width // HD
    summed = jnp.zeros(hidden.shape, jnp.float32)
    highest = []
    for group_idx in range(N_TENSOR):
        first_col = group_idx * group_width
        share_rows = low_back(hidden)
        projected = low(low_back(product('csd,ndk->ncsk', share_rows, weight_qkv[:, :, first_col:first_col + group_width])))
        shaped = projected.reshape(3, clip_count, FRAMES, PATCHES, heads_loc, HD)
        logits = low_back(product(forms[0], shaped[0], shaped[1]) * SCALE)
        highest.append(lax.optimization_barrier(jnp.max(logits, axis=(0, 1, 3, 4))))
        row_peak = lax.optimization_barrier(jnp.max(logits, axis=-1, keepdims=True))
        exponent = jnp.exp(logits - row_peak)
        weights = low(exponent / lax.optimization_barrier(jnp.sum(exponent, axis=-1, keepdims=True)))
        mixed_heads = low(low_back(product(forms[1], weights, shaped[2])))
        mixed_heads = mixed_heads.reshape(clip_count, seq_len, group_width)
        summed = summed + low(product('csk,kd->csd', mixed_heads, weight_out[first_col:first_col + group_width, :]))
    return (low_back(summed), jnp.concatenate(highest))

def feed_forward(hidden, weight_in, weight_out):
    group_width = weight_in.shape[1] // N_TENSOR
    summed = jnp.zeros(hidden.shape, jnp.float32)
    for group_idx in range(N_TENSOR):
        first_col = group_idx * group_width
        share_rows = low_back(hidden)
        pre_gelu = low_back(product('csd,df->csf', share_rows, weight_in[:, first_col:first_col + group_width]))
        active = low(jax.nn.gelu(pre_gelu, approximate=False))
        summed = summed + low(product('csf,fd->csd', active, weight_out[first_col:first_col + group_width, :]))
    return low_back(summed)

def layer(tokens, time_qkv, time_out, time_mixer, space_qkv, space_out, hidden_in, hidden_out, norm_gain, norm_bias):

    def pair_step(carry_in, row_block):
        normed_one = low(normalize(row_block, norm_gain[0], norm_bias[0]))
        mixer_in, time_high = attention(normed_one, time_qkv, time_out, TIME_FORMS)
        after_time = row_block + low_back(product('csd,de->cse', low(mixer_in), time_mixer))
        normed_two = low(normalize(after_time, norm_gain[1], norm_bias[1]))
        space_term, space_high = attention(normed_two, space_qkv, space_out, SPACE_FORMS)
        after_space = after_time + space_term
        normed_three = low(normalize(after_space, norm_gain[2], norm_bias[2]))
        result = after_space + feed_forward(normed_three, hidden_in, hidden_out)
        return (carry_in, (result, jnp.stack([time_high, space_high])))
    blocks = tokens.reshape(CLIPS // 2, 2, FRAMES * PATCHES, D)
    carry_out, outputs = lax.scan(jax.checkpoint(pair_step), jnp.zeros((), jnp.float32), blocks)
    return (outputs[0].reshape(tokens.shape), lax.optimization_barrier(jnp.max(outputs[1], axis=0)))

def reference(clip_tokens, time_qkv, time_out, time_mixer, space_qkv, space_out, hidden_in, hidden_out, norm_gain, norm_bias, cotangent):
    primals = tuple((source.astype(jnp.float32) for source in (clip_tokens, time_qkv, time_out, time_mixer, space_qkv, space_out, hidden_in, hidden_out, norm_gain, norm_bias)))
    result, pull_back, highs = jax.vjp(layer, *primals, has_aux=True)
    grads = pull_back(cotangent.astype(jnp.float32))
    qk_clip = jnp.sqrt(TAU / jnp.maximum(highs, TAU))
    return (result, grads[0], grads[1], grads[2], grads[3], grads[4], grads[5], grads[6], grads[7], grads[8], grads[9], qk_clip)
```

```python
import functools

import jax
import jax.numpy as jnp
from jax import lax
from jax.experimental import pallas as pl
from jax.experimental.pallas import tpu as pltpu
from jax.sharding import PartitionSpec as P

HD = 64
FRAMES = 8
PATCHES = 196
PAD = 208
SCALE = 0.125
TAU = 2.0
EPS = 1e-06
AXES = ("dp", "tensor")
F32 = jnp.float32
BF16 = jnp.bfloat16
VMEM_LIMIT = 60 * 1024 * 1024


def place(z, x, y, c):
    return ((z * 2 + x) * 2 + y) * 2 + c


ALL = [(z, x, y, c) for z in range(4) for x in range(2) for y in range(2) for c in range(2)]


def pairs(move, keep=lambda z, x, y, c: True):
    return [(place(*i), place(*move(*i))) for i in ALL if keep(*i)]


SWAP_C = pairs(lambda z, x, y, c: (z, x, y, 1 - c))
SWAP_Y = pairs(lambda z, x, y, c: (z, x, 1 - y, c))
SWAP_YC = pairs(lambda z, x, y, c: (z, x, 1 - y, 1 - c))
SWAP_X = pairs(lambda z, x, y, c: (z, 1 - x, y, c))
SWAP_Z1 = pairs(lambda z, x, y, c: (z ^ 1, x, y, c))
SWAP_Z2 = pairs(lambda z, x, y, c: (z ^ 2, x, y, c))
Z_MID = pairs(lambda z, x, y, c: (3 - z, x, y, c), lambda z, x, y, c: z in (1, 2))
Z_OUT = pairs(lambda z, x, y, c: (z ^ 1, x, y, c), lambda z, x, y, c: z in (1, 2))
Z_IN = pairs(lambda z, x, y, c: (z ^ 1, x, y, c), lambda z, x, y, c: z in (0, 3))


def send(value, route):
    return lax.ppermute(value, AXES, route)


def dot_nn(a, b):
    return lax.dot_general(a, b, (((1,), (0,)), ((), ())), preferred_element_type=F32)


def dot_nt(a, b):
    return lax.dot_general(a, b, (((1,), (1,)), ((), ())), preferred_element_type=F32)


def dot_tn(a, b):
    return lax.dot_general(a, b, (((0,), (0,)), ((), ())), preferred_element_type=F32)


def group_at(step):
    return jnp.where(step < 2, 2 * step + 1, 2 * step - 4)


def piece_of(r, rx, slot):
    base = (r % 2) * 5
    if r < 2:
        return (base + rx, slot)
    if rx == 0:
        return (base + 2, slot)
    return (base + 3, slot) if slot < 2 else (base + 4, slot - 2)


def slot_rows(where_ref):
    z = where_ref[0]
    low = z < 2
    return [z, z ^ 1, jnp.where(low, 2, 1), jnp.where(low, 3, 0)]


def start_loads(torus, where_ref, pieces, stores, sems):
    if not torus:
        for r in range(4):
            for b in range(2):
                pltpu.make_async_copy(pieces[0].at[r, b], stores[b].at[r], sems.at[r, b]).start()
        return
    x = where_ref[1]
    zs = slot_rows(where_ref)
    for i in range(4):
        r = (1, 3, 0, 2)[i]
        for rx in range(2):
            for slot in range(4):
                which, lead = piece_of(r, rx, slot)
                row = pl.multiple_of((zs[slot] * 2 + (x ^ rx)) * 96, 96)
                for b in range(2):
                    pltpu.make_async_copy(
                        pieces[which].at[lead, pl.ds(b * 96, 96), :],
                        stores[b].at[r, pl.ds(row, 96), :],
                        sems.at[r, b],
                    ).start()


def wait_loads(r, stores, sems):
    for b in range(2):
        pltpu.make_async_copy(stores[b].at[r], stores[b].at[r], sems.at[r, b]).wait()


def out_slot(torus, where_ref, dp):
    if not torus:
        return dp
    z_to, x_to = dp // 2, dp % 2
    far = ((where_ref[0] >> 1) ^ (z_to // 2)) * 2
    return (where_ref[1] ^ x_to) * 4 + far + z_to % 2


def normed(rows):
    mean = jnp.mean(rows, axis=-1, keepdims=True)
    centered = rows - mean
    inverse = lax.rsqrt(jnp.mean(centered * centered, axis=-1, keepdims=True) + EPS)
    return centered * inverse, inverse


def norm_back(dh, scaled, inverse, gain):
    weighted = dh * gain
    return inverse * (
        weighted
        - jnp.mean(weighted, axis=-1, keepdims=True)
        - scaled * jnp.mean(weighted * scaled, axis=-1, keepdims=True)
    )


def norm_sums(dh, scaled):
    gain = jnp.sum(dh * scaled, axis=0, keepdims=True)
    bias = jnp.sum(dh, axis=0, keepdims=True)
    return jnp.concatenate([gain, bias, jnp.zeros((6, dh.shape[1]), F32)], axis=0)


def blocks_of(space):
    return ((0, PAD), (PAD, PAD)) if space else ((0, 192), (192, 200))


def keep_mask(space, size):
    row = lax.broadcasted_iota(jnp.int32, (size, size), 0)
    col = lax.broadcasted_iota(jnp.int32, (size, size), 1)
    if space:
        return col < PATCHES
    return (row >> 3) == (col >> 3)


def head_lanes(size):
    lane = lax.broadcasted_iota(jnp.int32, (size, 192), 1)
    return [(lane >= j * HD) & (lane < (j + 1) * HD) for j in range(3)]


def attn_fwd_kernel(torus, space, norm, n_pieces, *refs):
    where_ref, x_ref, norms_ref = refs[:3]
    pieces = refs[3 : 3 + n_pieces]
    y_ref, q_ref, k_ref, v_ref, o_ref, high_ref = refs[3 + n_pieces : 9 + n_pieces]
    w_qk, w_vo, h_ref, sems = refs[9 + n_pieces :]
    step = pl.program_id(0)
    r = group_at(step)

    @pl.when(step == 0)
    def _():
        start_loads(torus, where_ref, pieces, (w_qk, w_vo), sems)
        scaled, _ = normed(x_ref[...].astype(F32))
        h_ref[...] = (scaled * norms_ref[norm : norm + 1] + norms_ref[3 + norm : 4 + norm]).astype(BF16)

    wait_loads(r, (w_qk, w_vo), sems)
    hidden = h_ref[...]
    qk = dot_nn(hidden, w_qk[r])
    w_two = w_vo[r]
    q_ref[0] = qk[:, :192].astype(BF16)
    k_ref[0] = qk[:, 192:].astype(BF16)
    v_ref[0] = dot_nn(hidden, w_two[:, :192]).astype(BF16)
    tops = [None, None, None]
    for start, size in blocks_of(space):
        q = q_ref[0, pl.ds(start, size), :]
        k = k_ref[0, pl.ds(start, size), :]
        v = v_ref[0, pl.ds(start, size), :]
        keep = keep_mask(space, size)
        lanes = head_lanes(size)
        mixed = None
        for j in range(3):
            logits = dot_nt(jnp.where(lanes[j], q, jnp.zeros_like(q)), k) * SCALE
            logits = jnp.where(keep, logits, -1e30)
            peak = jnp.max(logits, axis=-1, keepdims=True)
            exponent = jnp.exp(logits - peak)
            total = jnp.sum(exponent, axis=-1, keepdims=True)
            weights = (exponent * (1.0 / total)).astype(BF16)
            part = dot_nn(weights, v)
            mixed = part if mixed is None else jnp.where(lanes[j], part, mixed)
            if space:
                row = lax.broadcasted_iota(jnp.int32, (size, 1), 0)
                peak = jnp.where(row < PATCHES, peak, -1e30)
            top = jnp.max(peak, axis=0, keepdims=True)
            tops[j] = top if tops[j] is None else jnp.maximum(tops[j], top)
        o_ref[0, pl.ds(start, size), :] = mixed.astype(BF16)
    row8 = lax.broadcasted_iota(jnp.int32, (8, 128), 0)
    high = jnp.full((8, 128), -1e30, F32)
    for j in range(3):
        high = jnp.where(row8 == j, jnp.broadcast_to(tops[j], (8, 128)), high)
    high_ref[0] = high
    term = dot_nt(o_ref[0], w_two[:, 192:])

    @pl.when(step == 0)
    def _():
        y_ref[...] = term

    @pl.when(step > 0)
    def _():
        y_ref[...] += term


def whole(shape):
    return pl.BlockSpec(shape, lambda i: (0,) * len(shape))


def per_group(shape):
    return pl.BlockSpec((1,) + shape, lambda i: (group_at(i),) + (0,) * len(shape))


def attn_fwd(torus, space, norm, where, x, norms, pieces):
    n, width = x.shape
    kernel = functools.partial(attn_fwd_kernel, torus, space, norm, len(pieces))
    heads = jax.ShapeDtypeStruct((4, n, 192), BF16)
    return pl.pallas_call(
        kernel,
        grid=(4,),
        out_shape=(
            jax.ShapeDtypeStruct((n, width), F32),
            heads,
            heads,
            heads,
            heads,
            jax.ShapeDtypeStruct((4, 8, 128), F32),
        ),
        in_specs=[pl.BlockSpec(memory_space=pltpu.SMEM), whole((n, width)), whole(norms.shape)]
        + [pl.BlockSpec(memory_space=pl.ANY)] * len(pieces),
        out_specs=(whole((n, width)),)
        + (per_group((n, 192)),) * 4
        + (per_group((8, 128)),),
        scratch_shapes=[
            pltpu.VMEM((4, width, 384), BF16),
            pltpu.VMEM((4, width, 384), BF16),
            pltpu.VMEM((n, width), BF16),
            pltpu.SemaphoreType.DMA((4, 2)),
        ],
        compiler_params=pltpu.CompilerParams(vmem_limit_bytes=VMEM_LIMIT),
        cost_estimate=pl.CostEstimate(flops=3 * 10**9, bytes_accessed=12 * 10**6, transcendentals=10**6),
        name="attn_fwd_space" if space else "attn_fwd_time",
    )(where, x, norms, *pieces)


def attn_bwd_kernel(torus, space, norm, n_pieces, rows, *refs):
    where_ref, dy_in, x_ref, norms_ref, q_ref, k_ref, v_ref, o_ref = refs[:8]
    refs = refs[8:]
    mixer = rows > 192
    if mixer:
        dmix_ref = refs[0]
        refs = refs[1:]
    pieces = refs[:n_pieces]
    dx_ref, sums_ref, g0_ref, g1_ref = refs[n_pieces : n_pieces + 4]
    w_qk, w_vo, h_ref, scaled_ref, dh_ref, dy_ref, dq_ref, dk_ref, dv_ref, sems = refs[n_pieces + 4 :]
    step = pl.program_id(0)
    r = group_at(step)

    @pl.when(step == 0)
    def _():
        start_loads(torus, where_ref, pieces, (w_qk, w_vo), sems)
        scaled, _ = normed(x_ref[...].astype(F32))
        scaled_ref[...] = scaled
        h_ref[...] = (scaled * norms_ref[norm : norm + 1] + norms_ref[3 + norm : 4 + norm]).astype(BF16)
        dy_ref[...] = dy_in[...].astype(BF16)
        dh_ref[...] = jnp.zeros_like(dh_ref)

    wait_loads(r, (w_qk, w_vo), sems)
    dy = dy_ref[...]
    w_two = w_vo[r]
    dmixed = dot_nn(dy, w_two)[:, 192:].astype(BF16)
    dv_ref[...] = dmixed
    for start, size in blocks_of(space):
        q = q_ref[0, pl.ds(start, size), :]
        k = k_ref[0, pl.ds(start, size), :]
        v = v_ref[0, pl.ds(start, size), :]
        do = dv_ref[pl.ds(start, size), :]
        keep = keep_mask(space, size)
        lanes = head_lanes(size)
        dq = dk = dv = None
        for j in range(3):
            zero = jnp.zeros_like(q)
            logits = dot_nt(jnp.where(lanes[j], q, zero), k) * SCALE
            logits = jnp.where(keep, logits, -1e30)
            peak = jnp.max(logits, axis=-1, keepdims=True)
            exponent = jnp.exp(logits - peak)
            total = jnp.sum(exponent, axis=-1, keepdims=True)
            weights = exponent * (1.0 / total)
            dweights = dot_nt(jnp.where(lanes[j], do, zero), v)
            inner = jnp.sum(dweights * weights, axis=-1, keepdims=True)
            dlogits = (weights * (dweights - inner)).astype(BF16)
            dv_j = dot_tn(weights.astype(BF16), do)
            dq_j = dot_nn(dlogits, k)
            dk_j = dot_tn(dlogits, q)
            dq = dq_j if dq is None else jnp.where(lanes[j], dq_j, dq)
            dk = dk_j if dk is None else jnp.where(lanes[j], dk_j, dk)
            dv = dv_j if dv is None else jnp.where(lanes[j], dv_j, dv)
        dq_ref[pl.ds(start, size), :] = (dq * SCALE).astype(BF16)
        dk_ref[pl.ds(start, size), :] = (dk * SCALE).astype(BF16)
        dv_ref[pl.ds(start, size), :] = dv.astype(BF16)
    hidden = h_ref[...]
    dqk = jnp.concatenate([dq_ref[...], dk_ref[...]], axis=1)
    dv = dv_ref[...]
    dh_ref[...] += dot_nt(dqk, w_qk[r]) + dot_nt(dv, w_two[:, :192])
    g_qk = dot_tn(hidden, dqk).astype(BF16)
    g_vo = jnp.concatenate([dot_tn(hidden, dv), dot_tn(dy, o_ref[0])], axis=1).astype(BF16)

    def put(g_ref):
        for dp in range(8):
            slot = out_slot(torus, where_ref, dp)
            g_ref[0, slot, 0:96, :] = g_qk[dp * 96 : (dp + 1) * 96]
            g_ref[0, slot, 96:192, :] = g_vo[dp * 96 : (dp + 1) * 96]
            if mixer:
                t = where_ref[2] ^ r
                block = dmix_ref[pl.ds(pl.multiple_of(dp * 96 + t * 24, 8), 24), :]
                g_ref[0, slot, 192:240, :] = jnp.concatenate([block[:, :384], block[:, 384:]], axis=0).astype(BF16)

    @pl.when(step < 2)
    def _():
        put(g1_ref)

    @pl.when(step >= 2)
    def _():
        put(g0_ref)

    @pl.when(step == 3)
    def _():
        _, inverse = normed(x_ref[...].astype(F32))
        scaled = scaled_ref[...]
        dh = dh_ref[...]
        dx_ref[...] = norm_back(dh, scaled, inverse, norms_ref[norm : norm + 1]).astype(dx_ref.dtype)
        sums_ref[...] = norm_sums(dh, scaled)


def grad_specs(rows, lanes):
    shape = (1, 8, rows, lanes)
    last = (0, 0, 0)
    return (
        pl.BlockSpec(shape, lambda i: (jnp.maximum(i - 2, 0),) + last),
        pl.BlockSpec(shape, lambda i: (jnp.minimum(i, 1),) + last),
    )


def attn_bwd(torus, space, norm, where, dy, x, norms, saved, pieces, dmix=None, out_type=F32):
    n, width = x.shape
    rows = 192 if dmix is None else 240
    kernel = functools.partial(attn_bwd_kernel, torus, space, norm, len(pieces), rows)
    extra = [] if dmix is None else [dmix]
    grads = jax.ShapeDtypeStruct((2, 8, rows, 384), BF16)
    return pl.pallas_call(
        kernel,
        grid=(4,),
        out_shape=(
            jax.ShapeDtypeStruct((n, width), out_type),
            jax.ShapeDtypeStruct((8, width), F32),
            grads,
            grads,
        ),
        in_specs=[
            pl.BlockSpec(memory_space=pltpu.SMEM),
            whole((n, width)),
            whole((n, width)),
            whole(norms.shape),
        ]
        + [per_group((n, 192))] * 4
        + [whole(e.shape) for e in extra]
        + [pl.BlockSpec(memory_space=pl.ANY)] * len(pieces),
        out_specs=(whole((n, width)), whole((8, width))) + grad_specs(rows, 384),
        scratch_shapes=[
            pltpu.VMEM((4, width, 384), BF16),
            pltpu.VMEM((4, width, 384), BF16),
            pltpu.VMEM((n, width), BF16),
            pltpu.VMEM((n, width), F32),
            pltpu.VMEM((n, width), F32),
            pltpu.VMEM((n, width), BF16),
            pltpu.VMEM((n, 192), BF16),
            pltpu.VMEM((n, 192), BF16),
            pltpu.VMEM((n, 192), BF16),
            pltpu.SemaphoreType.DMA((4, 2)),
        ],
        compiler_params=pltpu.CompilerParams(vmem_limit_bytes=VMEM_LIMIT),
        cost_estimate=pl.CostEstimate(flops=7 * 10**9, bytes_accessed=20 * 10**6, transcendentals=10**6),
        name="attn_bwd_space" if space else "attn_bwd_time",
    )(where, dy, x, norms, *saved, *extra, *pieces)


def hidden_kernel(torus, n_pieces, *refs):
    where_ref, x_ref, norms_ref, ct_ref = refs[:4]
    pieces = refs[4 : 4 + n_pieces]
    out_ref, dx_ref, sums_ref, g0_ref, g1_ref = refs[4 + n_pieces : 9 + n_pieces]
    w_in, w_out, h_ref, scaled_ref, dh_ref, sems = refs[9 + n_pieces :]
    step = pl.program_id(0)
    r = group_at(step)

    @pl.when(step == 0)
    def _():
        start_loads(torus, where_ref, pieces, (w_in, w_out), sems)
        x = x_ref[...]
        scaled, _ = normed(x)
        scaled_ref[...] = scaled
        h_ref[...] = (scaled * norms_ref[2:3] + norms_ref[5:6]).astype(BF16)
        dh_ref[...] = jnp.zeros_like(dh_ref)
        out_ref[...] = x

    wait_loads(r, (w_in, w_out), sems)
    hidden = h_ref[...]
    ct = ct_ref[...]
    up, down = w_in[r], w_out[r]
    pre = dot_nn(hidden, up)
    bell = 0.5 * (1.0 + lax.erf(pre * 0.7071067811865476))
    active = (pre * bell).astype(BF16)
    slope = bell + pre * (jnp.exp(-0.5 * pre * pre) * 0.3989422804014327)
    dpre = (dot_nn(ct, down) * slope).astype(BF16)
    out_ref[...] += dot_nt(active, down)
    dh_ref[...] += dot_nt(dpre, up)
    g_in = dot_tn(hidden, dpre).astype(BF16)
    g_out = dot_tn(ct, active).astype(BF16)

    def put(g_ref):
        for dp in range(8):
            slot = out_slot(torus, where_ref, dp)
            g_ref[0, slot, 0:96, :] = g_in[dp * 96 : (dp + 1) * 96]
            g_ref[0, slot, 96:192, :] = g_out[dp * 96 : (dp + 1) * 96]

    @pl.when(step < 2)
    def _():
        put(g1_ref)

    @pl.when(step >= 2)
    def _():
        put(g0_ref)

    @pl.when(step == 3)
    def _():
        _, inverse = normed(x_ref[...])
        scaled = scaled_ref[...]
        dh = dh_ref[...]
        dx_ref[...] = ct_ref[...].astype(F32) + norm_back(dh, scaled, inverse, norms_ref[2:3])
        sums_ref[...] = norm_sums(dh, scaled)


def hidden_both(torus, where, x, norms, ct, pieces):
    n, width = x.shape
    kernel = functools.partial(hidden_kernel, torus, len(pieces))
    grads = jax.ShapeDtypeStruct((2, 8, 192, 768), BF16)
    return pl.pallas_call(
        kernel,
        grid=(4,),
        out_shape=(
            jax.ShapeDtypeStruct((n, width), F32),
            jax.ShapeDtypeStruct((n, width), F32),
            jax.ShapeDtypeStruct((8, width), F32),
            grads,
            grads,
        ),
        in_specs=[
            pl.BlockSpec(memory_space=pltpu.SMEM),
            whole((n, width)),
            whole(norms.shape),
            whole((n, width)),
        ]
        + [pl.BlockSpec(memory_space=pl.ANY)] * len(pieces),
        out_specs=(whole((n, width)), whole((n, width)), whole((8, width))) + grad_specs(192, 768),
        scratch_shapes=[
            pltpu.VMEM((4, width, 768), BF16),
            pltpu.VMEM((4, width, 768), BF16),
            pltpu.VMEM((n, width), BF16),
            pltpu.VMEM((n, width), F32),
            pltpu.VMEM((n, width), F32),
            pltpu.SemaphoreType.DMA((4, 2)),
        ],
        compiler_params=pltpu.CompilerParams(vmem_limit_bytes=VMEM_LIMIT),
        cost_estimate=pl.CostEstimate(flops=12 * 10**9, bytes_accessed=25 * 10**6, transcendentals=3 * 10**6),
        name="hidden_both",
    )(where, x, norms, ct, *pieces)


def place_kernel(n_pieces, *refs):
    where_ref = refs[0]
    pieces = refs[1 : 1 + n_pieces]
    mixer_ref, norms_ref, held = refs[1 + n_pieces :]
    x = where_ref[1]
    zs = slot_rows(where_ref)
    left = jnp.zeros((8, 384), F32)
    right = jnp.zeros((8, 384), F32)
    for r in range(4):
        t = where_ref[2] ^ r
        for rx in range(2):
            for slot in range(4):
                which, lead = piece_of(r, rx, slot)
                row = pl.multiple_of((zs[slot] * 2 + (x ^ rx)) * 96 + t * 24, 8)
                tail = pieces[which][lead].astype(F32)
                held[pl.ds(row, 24), 0:384] = tail[0:24]
                held[pl.ds(row, 24), 384:768] = tail[24:48]
                left = left + tail[48:56]
                right = right + tail[56:64]
    norms_ref[...] = jnp.concatenate([left, right], axis=1)
    mixer_ref[...] = held[...].astype(BF16)


def place_mixer(where, pieces):
    return pl.pallas_call(
        functools.partial(place_kernel, len(pieces)),
        grid=(1,),
        out_shape=(jax.ShapeDtypeStruct((768, 768), BF16), jax.ShapeDtypeStruct((8, 768), F32)),
        in_specs=[pl.BlockSpec(memory_space=pltpu.SMEM)]
        + [pl.BlockSpec((p.shape[0], 64, 384), lambda i: (0, 3, 0)) for p in pieces],
        out_specs=(whole((768, 768)), whole((8, 768))),
        scratch_shapes=[pltpu.VMEM((768, 768), F32)],
        compiler_params=pltpu.CompilerParams(vmem_limit_bytes=VMEM_LIMIT),
        cost_estimate=pl.CostEstimate(flops=10**6, bytes_accessed=4 * 10**6, transcendentals=0),
        name="place_mixer",
    )(where, *pieces)


def gather_pieces(shard, inner):
    pair = jnp.stack([shard, send(shard, SWAP_Z1)])
    middle = send(pair, Z_MID)
    outer = send(middle, Z_OUT)
    own = jnp.concatenate([pair, jnp.where(inner, middle, outer)], axis=0)
    by_x = send(own, SWAP_X)
    by_y = send(own, SWAP_Y)
    both_a = send(by_x[:2], SWAP_Y)
    both_b = send(by_y[2:], SWAP_X)
    five = [own, by_x, by_y, both_a, both_b]
    return five + [send(v, SWAP_C) for v in five]


def plus(a, b):
    return (a.astype(F32) + b.astype(F32)).astype(BF16)


def reduce_pieces(g_keep, g_send, z):
    held = plus(g_keep, send(g_send, SWAP_C))
    own, by_x, by_y, both = held[0, :4], held[0, 4:], held[1, :4], held[1, 4:]
    got_a = send(both[:2], SWAP_Y)
    got_b = send(both[2:], SWAP_X)
    by_x = jnp.concatenate([plus(by_x[:2], got_a), by_x[2:]], axis=0)
    by_y = jnp.concatenate([by_y[:2], plus(by_y[2:], got_b)], axis=0)
    own = (
        own.astype(F32) + send(by_x, SWAP_X).astype(F32) + send(by_y, SWAP_Y).astype(F32)
    ).astype(BF16)
    near, far = own[:2], own[2:]
    far = plus(far, send(far, Z_IN))
    near = plus(near, send(far, Z_MID))
    low = (z & 1) == 0
    mine = jnp.where(low, near[0], near[1])
    other = jnp.where(low, near[1], near[0])
    return mine.astype(F32) + send(other, SWAP_Z1).astype(F32)


def pack_attn(w_qkv, w_out):
    top = jnp.concatenate([w_qkv[0], w_qkv[1]], axis=1)
    low = jnp.concatenate([w_qkv[2], w_out.T], axis=1)
    return jnp.stack([top, low])


def unpack_attn(piece):
    grad_qkv = jnp.stack([piece[0, :, :192], piece[0, :, 192:], piece[1, :, :192]])
    return grad_qkv, piece[1, :, 192:].T


def full_gather(packed):
    return lax.all_gather(lax.all_gather(packed, "dp", axis=1, tiled=True), "tensor", axis=0)


def full_reduce(g_keep, g_send):
    rows, lanes = g_keep.shape[2:]
    full = jnp.stack([g_keep[0], g_send[0], g_keep[1], g_send[1]]).reshape(4, 8, 2, rows // 2, lanes)
    full = full.transpose(0, 2, 1, 3, 4).reshape(4, 2, 4 * rows, lanes).astype(F32)
    mine = lax.psum_scatter(full, "tensor", scatter_dimension=0, tiled=False)
    return lax.psum_scatter(mine, "dp", scatter_dimension=1, tiled=True)


def exchange(torus, groups, t):
    if not torus:
        return lax.all_to_all(groups, "tensor", 0, 0, tiled=True)
    routes = (SWAP_C, SWAP_Y, SWAP_YC)
    got = [groups[0]] + [send(groups[i + 1], routes[i]) for i in range(3)]
    return jnp.stack(got)


def reorder(torus, groups, t):
    if not torus:
        return groups
    swap_c = (t & 1) == 1
    swap_y = (t >> 1) == 1
    groups = jnp.where(swap_c, jnp.stack([groups[1], groups[0], groups[3], groups[2]]), groups)
    return jnp.where(swap_y, jnp.stack([groups[2], groups[3], groups[0], groups[1]]), groups)


def to_patches(torus, rows, t):
    width = rows.shape[-1]
    groups = rows.reshape(2, 4, 49, width).transpose(1, 0, 2, 3)
    got = exchange(torus, reorder(torus, groups, t), t)
    return got.transpose(2, 0, 1, 3).reshape(392, width)


def to_frames(torus, rows, t):
    width = rows.shape[-1]
    groups = rows.reshape(49, 4, 2, width).transpose(1, 2, 0, 3)
    got = reorder(torus, exchange(torus, groups, t), t)
    return got.transpose(1, 0, 2, 3).reshape(2, PATCHES, width)


def padded(frames):
    return jnp.pad(frames, ((0, 0), (0, PAD - PATCHES), (0, 0))).reshape(2 * PAD, -1)


def trimmed(rows):
    return rows.reshape(2, PAD, -1)[:, :PATCHES]


def shards(
    torus,
    dp_size,
    clip_tokens,
    time_qkv,
    time_out,
    time_mixer,
    space_qkv,
    space_out,
    hidden_in,
    hidden_out,
    norm_gain,
    norm_bias,
    cotangent,
):
    dp = lax.axis_index("dp")
    t = lax.axis_index("tensor")
    z, x = dp >> 1, dp & 1
    where = jnp.stack([z, x, t, t]).astype(jnp.int32)
    width = clip_tokens.shape[-1]
    tokens = clip_tokens[0]
    ct = padded(cotangent[0].reshape(2, PATCHES, width))
    base = padded(tokens.reshape(2, PATCHES, width)).astype(F32)
    by_patch = to_patches(torus, tokens, t)

    time_w = pack_attn(time_qkv, time_out)
    space_w = pack_attn(space_qkv, space_out)
    ff_w = jnp.stack([hidden_in, hidden_out.T])
    norm_rows = jnp.concatenate([norm_gain, norm_bias], axis=0)
    share = norm_rows.shape[1]
    if torus:
        inner = (z == 1) | (z == 2)
        spread = lax.dynamic_update_slice(
            jnp.zeros((8, width), BF16), norm_rows, (0, (dp * 4 + t) * share)
        )
        time_shard = jnp.concatenate(
            [
                time_w.reshape(192, 384),
                time_mixer[:, :384],
                time_mixer[:, 384:],
                spread[:, :384],
                spread[:, 384:],
            ],
            axis=0,
        )
        time_p = gather_pieces(time_shard, inner)
        space_p = gather_pieces(space_w.reshape(192, 384), inner)
        ff_p = gather_pieces(ff_w.reshape(192, 768), inner)
        mixer, norms = place_mixer(where, time_p)
    else:
        time_p = [full_gather(time_w)]
        space_p = [full_gather(space_w)]
        ff_p = [full_gather(ff_w)]
        mixer = lax.all_gather(time_mixer, AXES, axis=0, tiled=True)
        norms = lax.all_gather(norm_rows, AXES, axis=1, tiled=True).astype(F32)
        norms = jnp.pad(norms, ((0, 2), (0, 0)))

    y_time, *kept_time, high_time = attn_fwd(torus, False, 0, where, by_patch, norms, time_p)
    mixer_in = padded(to_frames(torus, y_time.astype(BF16), t))
    after_time = base + jnp.dot(mixer_in, mixer, preferred_element_type=F32)
    y_space, *kept_space, high_space = attn_fwd(torus, True, 1, where, after_time, norms, space_p)
    after_space = after_time + y_space
    out_rows, d_space, sums_three, g0_ff, g1_ff = hidden_both(
        torus, where, after_space, norms, ct, ff_p
    )
    dln_two, sums_two, g0_space, g1_space = attn_bwd(
        torus, True, 1, where, d_space, after_time, norms, kept_space, space_p
    )
    d_time = d_space + dln_two
    d_time_low = d_time.astype(BF16)
    dmix = lax.dot_general(
        mixer_in, d_time_low, (((0,), (0,)), ((), ())), preferred_element_type=F32
    )
    d_mixer_in = lax.dot_general(
        d_time_low, mixer, (((1,), (1,)), ((), ())), preferred_element_type=F32
    ).astype(BF16)
    d_patch = to_patches(torus, trimmed(d_mixer_in).reshape(392, width), t)
    dln_one, sums_one, g0_time, g1_time = attn_bwd(
        torus,
        False,
        0,
        where,
        d_patch,
        by_patch,
        norms,
        kept_time,
        time_p,
        dmix=dmix if torus else None,
        out_type=BF16,
    )
    back = to_frames(torus, dln_one, t).astype(F32)
    input_grad = trimmed(d_time) + back

    highs = jnp.stack([high_time[:, :3, 0], high_space[:, :3, 0]], axis=1)
    sums = jnp.concatenate(
        [sums_one[:1], sums_two[:1], sums_three[:1], sums_one[1:2], sums_two[1:2], sums_three[1:2]]
    )
    if torus:
        ff = reduce_pieces(g0_ff, g1_ff, z).reshape(2, 96, 768)
        space = reduce_pieces(g0_space, g1_space, z).reshape(2, 96, 384)
        timed = reduce_pieces(g0_time, g1_time, z)
        mixer_grad = jnp.concatenate([timed[192:216], timed[216:240]], axis=1)
        timed = timed[:192].reshape(2, 96, 384)
        for route, flip in ((SWAP_C, 1), (SWAP_Y, 2), (SWAP_X, 0), (SWAP_Z1, 0), (SWAP_Z2, 0)):
            other = send(highs, route)
            highs = jnp.maximum(highs, jnp.stack([other[i ^ flip] for i in range(4)]))
            sums = sums + send(sums, route)
        highest = highs[0]
        mine = lax.dynamic_slice(sums, (0, (dp * 4 + t) * share), (6, share))
    else:
        ff = full_reduce(g0_ff, g1_ff)
        space = full_reduce(g0_space, g1_space)
        timed = full_reduce(g0_time, g1_time)
        mixer_grad = lax.psum_scatter(dmix, AXES, scatter_dimension=0, tiled=True)
        highest = lax.dynamic_index_in_dim(lax.pmax(highs, AXES), t, 0, keepdims=False)
        mine = lax.psum_scatter(sums, AXES, scatter_dimension=1, tiled=True)
    qk_clip = jnp.sqrt(TAU / jnp.maximum(highest, TAU))
    time_qkv_grad, time_out_grad = unpack_attn(timed)
    space_qkv_grad, space_out_grad = unpack_attn(space)
    return (
        trimmed(out_rows).reshape(1, 392, width),
        input_grad.reshape(1, 392, width),
        time_qkv_grad,
        time_out_grad,
        mixer_grad,
        space_qkv_grad,
        space_out_grad,
        ff[0],
        ff[1].T,
        mine[:3],
        mine[3:],
        qk_clip,
    )


def solution(mesh):
    sizes = dict(mesh.shape)
    torus = sizes["dp"] == 8 and sizes["tensor"] == 4
    in_specs = (
        P("dp", "tensor", None),
        P(None, "dp", "tensor"),
        P("tensor", "dp"),
        P(("dp", "tensor"), None),
        P(None, "dp", "tensor"),
        P("tensor", "dp"),
        P("dp", "tensor"),
        P("tensor", "dp"),
        P(None, ("dp", "tensor")),
        P(None, ("dp", "tensor")),
        P("dp", "tensor", None),
    )
    out_specs = (
        P("dp", "tensor", None),
        P("dp", "tensor", None),
        P(None, "dp", "tensor"),
        P("tensor", "dp"),
        P(("dp", "tensor"), None),
        P(None, "dp", "tensor"),
        P("tensor", "dp"),
        P("dp", "tensor"),
        P("tensor", "dp"),
        P(None, ("dp", "tensor")),
        P(None, ("dp", "tensor")),
        P(None, "tensor"),
    )
    body = functools.partial(shards, torus, sizes["dp"])
    return jax.shard_map(body, mesh=mesh, in_specs=in_specs, out_specs=out_specs, check_vma=False)
```

```python
import functools

import jax
import jax.numpy as jnp
from jax import lax
from jax.experimental import pallas as pl
from jax.experimental.pallas import tpu as pltpu
from jax.sharding import PartitionSpec as P

HD = 64
FRAMES = 8
PATCHES = 196
PAD = 208
SCALE = 0.125
TAU = 2.0
EPS = 1e-06
AXES = ("dp", "tensor")
F32 = jnp.float32
BF16 = jnp.bfloat16
PIECE = 112
VMEM_LIMIT = 60 * 1024 * 1024


def place(z, x, y, c):
    return ((z * 2 + x) * 2 + y) * 2 + c


ALL = [(z, x, y, c) for z in range(4) for x in range(2) for y in range(2) for c in range(2)]


def pairs(move, keep=lambda z, x, y, c: True):
    return [(place(*i), place(*move(*i))) for i in ALL if keep(*i)]


SWAP_C = pairs(lambda z, x, y, c: (z, x, y, 1 - c))
SWAP_Y = pairs(lambda z, x, y, c: (z, x, 1 - y, c))
SWAP_YC = pairs(lambda z, x, y, c: (z, x, 1 - y, 1 - c))
SWAP_X = pairs(lambda z, x, y, c: (z, 1 - x, y, c))
SWAP_Z1 = pairs(lambda z, x, y, c: (z ^ 1, x, y, c))
SWAP_Z2 = pairs(lambda z, x, y, c: (z ^ 2, x, y, c))
SIDE_ONE = pairs(lambda z, x, y, c: (z, x, 1 - y, c) if c else (z, 1 - x, y, c))
SIDE_TWO = pairs(lambda z, x, y, c: (z, 1 - x, y, c) if c else (z, x, 1 - y, c))


def send(value, route):
    return lax.ppermute(value, AXES, route)


def dot_nn(a, b):
    return lax.dot_general(a, b, (((1,), (0,)), ((), ())), preferred_element_type=F32)


def dot_nt(a, b):
    return lax.dot_general(a, b, (((1,), (1,)), ((), ())), preferred_element_type=F32)


def dot_tn(a, b):
    return lax.dot_general(a, b, (((0,), (0,)), ((), ())), preferred_element_type=F32)


def block_at(where_ref, which, lead):
    rc, block, slot = which // 2, (which % 2) * 2 + lead // 4, lead % 4
    low, high = block & 1, block >> 1
    first = ((where_ref[2] ^ rc) & 1) == 0
    rx = jnp.where(first, low, high)
    ry = jnp.where(first, high, low)
    return rc, ry, (where_ref[0] ^ slot) * 2 + (where_ref[1] ^ rx)


def start_loads(torus, where_ref, pieces, stores, sems, groups):
    if not torus:
        for i, r in enumerate(groups):
            for b in range(2):
                pltpu.make_async_copy(pieces[0].at[r, b], stores[b].at[i], sems.at[i, b]).start()
        return
    every = len(groups) == 4
    both = (2, 3) if groups[0] == 1 else (0, 1)
    for at, which in enumerate(range(4) if every else both):
        for lead in range(8):
            rc, ry, dp = block_at(where_ref, which, lead)
            i = ry * 2 + rc if every else ry
            row = pl.multiple_of(dp * 96, 96)
            for b in range(2):
                pltpu.make_async_copy(
                    pieces[which if every else at].at[lead, pl.ds(b * 96, 96), :],
                    stores[b].at[i, pl.ds(row, 96), :],
                    sems.at[i, b],
                ).start()


def wait_loads(i, stores, sems):
    for b in range(2):
        pltpu.make_async_copy(stores[b].at[i], stores[b].at[i], sems.at[i, b]).wait()


def out_block(torus, where_ref, rc, step, dp):
    if not torus:
        return step * 8 + dp
    slot = where_ref[0] ^ (dp // 2)
    rx, ry = where_ref[1] ^ (dp % 2), step
    first = ((where_ref[2] ^ rc) & 1) == 0
    return jnp.where(first, ry, rx) * 8 + jnp.where(first, rx, ry) * 4 + slot


def peer(torus, where_ref, r):
    return where_ref[2] ^ r if torus else r


def put_grads(torus, where_ref, rc, step, stage, g_ref, sem, first, second, third=None):
    for dp in range(8):
        stage[step, dp, 0:96, :] = first[dp * 96 : (dp + 1) * 96]
        stage[step, dp, 96:192, :] = second[dp * 96 : (dp + 1) * 96]
        if third is not None:
            stage[step, dp, 192:, :] = third[dp]
        block = out_block(torus, where_ref, rc, step, dp)
        pltpu.make_async_copy(stage.at[step, dp], g_ref.at[block], sem.at[step]).start()


def wait_grads(stage, sem):
    for i in range(2):
        pltpu.make_async_copy(stage.at[i], stage.at[i], sem.at[i]).wait()


def normed(rows):
    mean = jnp.mean(rows, axis=-1, keepdims=True)
    centered = rows - mean
    inverse = lax.rsqrt(jnp.mean(centered * centered, axis=-1, keepdims=True) + EPS)
    return centered * inverse, inverse


def norm_low(scaled, norms_ref, norm):
    return (scaled * norms_ref[norm : norm + 1] + norms_ref[3 + norm : 4 + norm]).astype(BF16)


def norm_back(dh, scaled, inverse, gain):
    weighted = dh * gain
    return inverse * (
        weighted
        - jnp.mean(weighted, axis=-1, keepdims=True)
        - scaled * jnp.mean(weighted * scaled, axis=-1, keepdims=True)
    )


def norm_sums(dh, scaled):
    gain = jnp.sum(dh * scaled, axis=0, keepdims=True)
    bias = jnp.sum(dh, axis=0, keepdims=True)
    return jnp.concatenate([gain, bias, jnp.zeros((6, dh.shape[1]), F32)], axis=0)


def ones_at(chosen):
    return jnp.where(chosen, 1.0, 0.0).astype(BF16)


def time_rows(r):
    row = lax.broadcasted_iota(jnp.int32, (PIECE, 392), 0)
    col = lax.broadcasted_iota(jnp.int32, (PIECE, 392), 1)
    return ones_at((((col >> 1) & 3) == r) & (row == (col & 1) * 49 + (col >> 3)))


def frame_rows(group):
    row = lax.broadcasted_iota(jnp.int32, (PIECE, 2 * PAD), 0)
    col = lax.broadcasted_iota(jnp.int32, (PIECE, 2 * PAD), 1)
    second = jnp.where(col >= PAD, 1, 0)
    patch = col - second * PAD - group * 49
    return ones_at((patch >= 0) & (patch < 49) & (row == second * 49 + patch))


def blocks_of(space):
    return ((0, PAD), (PAD, PAD)) if space else ((0, 192), (192, 200))


def keep_mask(space, size):
    row = lax.broadcasted_iota(jnp.int32, (size, size), 0)
    col = lax.broadcasted_iota(jnp.int32, (size, size), 1)
    if space:
        return row < PATCHES
    return (row >> 3) == (col >> 3)


def head_lanes(size):
    lane = lax.broadcasted_iota(jnp.int32, (size, 192), 1)
    return [(lane >= j * HD) & (lane < (j + 1) * HD) for j in range(3)]


def whole(shape):
    return pl.BlockSpec(shape, lambda i: (0,) * len(shape))


def raw():
    return pl.BlockSpec(memory_space=pl.ANY)


def scalars():
    return pl.BlockSpec(memory_space=pltpu.SMEM)


def like(*shape, dtype=F32):
    return jax.ShapeDtypeStruct(shape, dtype)


def cost(flops, size, exps):
    return pl.CostEstimate(flops=flops, bytes_accessed=size, transcendentals=exps)


PARAMS = pltpu.CompilerParams(vmem_limit_bytes=VMEM_LIMIT)


def heads_fwd(space, hidden, w_qk, w_vo, q_ref, k_ref, v_ref, o_ref, high_ref):
    qk = dot_nn(hidden, w_qk)
    q_ref[0] = qk[:, :192].astype(BF16)
    k_ref[0] = qk[:, 192:].astype(BF16)
    v_ref[0] = dot_nn(hidden, w_vo[:, :192]).astype(BF16)
    tops = [None, None, None]
    for start, size in blocks_of(space):
        q = q_ref[0, pl.ds(start, size), :]
        k = k_ref[0, pl.ds(start, size), :]
        v = v_ref[0, pl.ds(start, size), :]
        keep = keep_mask(space, size)
        zero = jnp.zeros_like(q)
        q = q * jnp.asarray(SCALE, BF16)
        mixed = None
        for j, mine in enumerate(head_lanes(size)):
            logits = jnp.where(keep, dot_nt(k, jnp.where(mine, q, zero)), -1e30)
            peak = jnp.max(logits, axis=0, keepdims=True)
            exponent = jnp.exp(logits - peak)
            weights = (exponent * (1.0 / jnp.sum(exponent, axis=0, keepdims=True))).astype(BF16)
            part = dot_tn(weights, jnp.where(mine, v, zero))
            mixed = part if mixed is None else mixed + part
            if space:
                col = lax.broadcasted_iota(jnp.int32, (1, size), 1)
                peak = jnp.where(col < PATCHES, peak, -1e30)
            top = jnp.max(peak, axis=1, keepdims=True)
            tops[j] = top if tops[j] is None else jnp.maximum(tops[j], top)
        o_ref[0, pl.ds(start, size), :] = mixed.astype(BF16)
    row8 = lax.broadcasted_iota(jnp.int32, (8, 128), 0)
    high = jnp.full((8, 128), -1e30, F32)
    for j in range(3):
        high = jnp.where(row8 == j, jnp.broadcast_to(tops[j], (8, 128)), high)
    high_ref[0] = high
    return dot_nt(o_ref[0], w_vo[:, 192:])


def time_fwd_kernel(torus, n_pieces, n_deps, where_ref, x_ref, norms_ref, *refs):
    pieces, refs = refs[:n_pieces], refs[n_pieces + n_deps :]
    outs, saved, refs = refs[:4], refs[4:9], refs[9:]
    w_qk, w_vo, h_ref, y_ref, sems = refs
    r = pl.program_id(0)

    @pl.when(r == 0)
    def _():
        start_loads(torus, where_ref, pieces, (w_qk, w_vo), sems, range(4))
        h_ref[...] = norm_low(normed(x_ref[...].astype(F32))[0], norms_ref, 0)
        y_ref[...] = jnp.zeros_like(y_ref)

    wait_loads(r, (w_qk, w_vo), sems)
    y_ref[...] += heads_fwd(False, h_ref[...], w_qk[r], w_vo[r], *saved)

    @pl.when(r == 3)
    def _():
        low = y_ref[...].astype(BF16)
        for i in range(4):
            outs[i][...] = dot_nn(time_rows(i), low).astype(BF16)


def space_fwd_kernel(torus, n_pieces, n_deps, where_ref, base_ref, norms_ref, mixer_ref, y0, y1, y2, y3, *refs):
    pieces, refs = refs[:n_pieces], refs[n_pieces + n_deps :]
    x2_ref, x1_ref, mixer_in_ref = refs[:3]
    saved, refs = refs[3:8], refs[8:]
    w_qk, w_vo, h_ref, sems = refs
    r = pl.program_id(0)

    @pl.when(r == 0)
    def _():
        start_loads(torus, where_ref, pieces, (w_qk, w_vo), sems, range(4))
        placed = None
        for i, piece in enumerate((y0, y1, y2, y3)):
            part = dot_tn(frame_rows(peer(torus, where_ref, i)), piece[...])
            placed = part if placed is None else placed + part
        mixer_in = placed.astype(BF16)
        mixer_in_ref[...] = mixer_in
        x1 = base_ref[...].astype(F32) + dot_nn(mixer_in, mixer_ref[...])
        x1_ref[...] = x1
        x2_ref[...] = x1
        h_ref[...] = norm_low(normed(x1)[0], norms_ref, 1)

    wait_loads(r, (w_qk, w_vo), sems)
    x2_ref[...] += heads_fwd(True, h_ref[...], w_qk[r], w_vo[r], *saved)


def per_group(shape, first=0, step=1):
    return pl.BlockSpec((1,) + shape, lambda i: (first + step * i,) + (0,) * len(shape))


def kept_shapes(n):
    return (like(4, n, 192, dtype=BF16),) * 4 + (like(4, 8, 128),)


def kept_specs(n):
    return (per_group((n, 192)),) * 4 + (per_group((8, 128)),)


def half(torus, pieces, rc):
    return pieces[2 * rc : 2 * rc + 2] if torus else pieces


def attn_stores(groups, width):
    return [
        pltpu.VMEM((groups, width, 384), BF16),
        pltpu.VMEM((groups, width, 384), BF16),
    ]


def time_fwd(torus, where, x, norms, pieces, deps):
    n, width = x.shape
    outs = pl.pallas_call(
        functools.partial(time_fwd_kernel, torus, len(pieces), len(deps)),
        grid=(4,),
        out_shape=(like(PIECE, width, dtype=BF16),) * 4 + kept_shapes(n),
        in_specs=[scalars(), whole(x.shape), whole(norms.shape)]
        + [raw()] * (len(pieces) + len(deps)),
        out_specs=(whole((PIECE, width)),) * 4 + kept_specs(n),
        scratch_shapes=attn_stores(4, width)
        + [
            pltpu.VMEM((n, width), BF16),
            pltpu.VMEM((n, width), F32),
            pltpu.SemaphoreType.DMA((4, 2)),
        ],
        compiler_params=PARAMS,
        cost_estimate=cost(3 * 10**9, 12 * 10**6, 10**6),
        name="time_fwd",
    )(where, x, norms, *pieces, *deps)
    return list(outs[:4]), list(outs[4:8]), outs[8]


def space_fwd(torus, where, base, norms, mixer, y_pieces, pieces, deps):
    n, width = base.shape
    outs = pl.pallas_call(
        functools.partial(space_fwd_kernel, torus, len(pieces), len(deps)),
        grid=(4,),
        out_shape=(like(n, width), like(n, width), like(n, width, dtype=BF16)) + kept_shapes(n),
        in_specs=[scalars(), whole(base.shape), whole(norms.shape), whole(mixer.shape)]
        + [whole((PIECE, width))] * 4
        + [raw()] * (len(pieces) + len(deps)),
        out_specs=(whole((n, width)),) * 3 + kept_specs(n),
        scratch_shapes=attn_stores(4, width)
        + [pltpu.VMEM((n, width), BF16), pltpu.SemaphoreType.DMA((4, 2))],
        compiler_params=PARAMS,
        cost_estimate=cost(3 * 10**9, 12 * 10**6, 10**6),
        name="space_fwd",
    )(where, base, norms, mixer, *y_pieces, *pieces, *deps)
    return outs[0], outs[1], outs[2], list(outs[3:7]), outs[7]


def heads_bwd(space, dy, hidden, w_qk, w_vo, q_ref, k_ref, v_ref, o_ref, dq_ref, dk_ref, dv_ref):
    dv_ref[...] = dot_nn(dy, w_vo)[:, 192:].astype(BF16)
    for start, size in blocks_of(space):
        q = q_ref[0, pl.ds(start, size), :]
        k = k_ref[0, pl.ds(start, size), :]
        v = v_ref[0, pl.ds(start, size), :]
        do = dv_ref[pl.ds(start, size), :]
        keep = keep_mask(space, size)
        zero = jnp.zeros_like(q)
        q = q * jnp.asarray(SCALE, BF16)
        dq = dk = dv = None
        for mine in head_lanes(size):
            q_j = jnp.where(mine, q, zero)
            do_j = jnp.where(mine, do, zero)
            logits = jnp.where(keep, dot_nt(k, q_j), -1e30)
            exponent = jnp.exp(logits - jnp.max(logits, axis=0, keepdims=True))
            weights = exponent * (1.0 / jnp.sum(exponent, axis=0, keepdims=True))
            dweights = dot_nt(v, do_j)
            inner = jnp.sum(dweights * weights, axis=0, keepdims=True)
            dlogits = (weights * (dweights - inner)).astype(BF16)
            dv_j = dot_nn(weights.astype(BF16), do_j)
            dk_j = dot_nn(dlogits, q_j)
            dq_j = dot_tn(dlogits, jnp.where(mine, k, zero))
            dq = dq_j if dq is None else dq + dq_j
            dk = dk_j if dk is None else dk + dk_j
            dv = dv_j if dv is None else dv + dv_j
        dq_ref[pl.ds(start, size), :] = (dq * SCALE).astype(BF16)
        dk_ref[pl.ds(start, size), :] = dk.astype(BF16)
        dv_ref[pl.ds(start, size), :] = dv.astype(BF16)
    dqk = jnp.concatenate([dq_ref[...], dk_ref[...]], axis=1)
    dv = dv_ref[...]
    dh = dot_nt(dqk, w_qk) + dot_nt(dv, w_vo[:, :192])
    g_qk = dot_tn(hidden, dqk).astype(BF16)
    g_vo = jnp.concatenate([dot_tn(hidden, dv), dot_tn(dy, o_ref[0])], axis=1).astype(BF16)
    return dh, g_qk, g_vo


def bwd_kernel(torus, space, part, n_pieces, n_deps, where_ref, *refs):
    norm = 1 if space else 0
    last = part == 1
    n_dy = 1 if space or last else 4
    dy_in, refs = refs[:n_dy], refs[n_dy:]
    x_ref, norms_ref = refs[:2]
    kept, refs = refs[2:6], refs[6:]
    if last:
        dh_in, refs = refs[0], refs[1:]
    if space and last:
        mixer_in_ref, mixer_ref = refs[:2]
        refs = refs[2:]
    if not space:
        dmix_ref, refs = refs[0], refs[1:]
    pieces, refs = refs[:n_pieces], refs[n_pieces + n_deps :]
    g_ref, refs = refs[0], refs[1:]
    if not last:
        dh_out, refs = refs[0], refs[1:]
        if not space:
            dy_out, refs = refs[0], refs[1:]
    else:
        sums_ref, refs = refs[0], refs[1:]
        if space:
            d_ref, dmix_out = refs[:2]
            refs = refs[2:]
        outs, refs = refs[:4], refs[4:]
    w_qk, w_vo, h_ref, dy_ref, dq_ref, dk_ref, dv_ref, dh_ref, stage, sems, g_sem = refs
    step = pl.program_id(0)
    r = 2 * step + (1 - part)

    @pl.when(step == 0)
    def _():
        start_loads(torus, where_ref, pieces, (w_qk, w_vo), sems, (0, 2) if last else (1, 3))
        h_ref[...] = norm_low(normed(x_ref[...].astype(F32))[0], norms_ref, norm)
        if n_dy == 1:
            dy_ref[...] = dy_in[0][...].astype(BF16)
        else:
            placed = None
            for i in range(4):
                term = dot_tn(time_rows(i), dy_in[i][...])
                placed = term if placed is None else placed + term
            dy_ref[...] = placed.astype(BF16)
            dy_out[...] = placed.astype(BF16)
        dh_ref[...] = dh_in[...] if last else jnp.zeros_like(dh_ref)

    wait_loads(step, (w_qk, w_vo), sems)
    dh, g_qk, g_vo = heads_bwd(
        space, dy_ref[...], h_ref[...], w_qk[step], w_vo[step], *kept, dq_ref, dk_ref, dv_ref
    )
    dh_ref[...] += dh
    third = None
    if not space and torus:
        t = where_ref[2] ^ r
        third = []
        for dp in range(8):
            block = dmix_ref[pl.ds(pl.multiple_of(dp * 96 + t * 24, 8), 24), :]
            block = jnp.concatenate([block[:, :384], block[:, 384:], jnp.zeros((16, 384), F32)], axis=0)
            third.append(block.astype(BF16))
    put_grads(torus, where_ref, 1 - part, step, stage, g_ref, g_sem, g_qk, g_vo, third)

    @pl.when(step == 1)
    def _():
        if not last:
            dh_out[...] = dh_ref[...]
            wait_grads(stage, g_sem)
            return
        scaled, inverse = normed(x_ref[...].astype(F32))
        total = dh_ref[...]
        sums_ref[...] = norm_sums(total, scaled)
        dx = norm_back(total, scaled, inverse, norms_ref[norm : norm + 1])
        if space:
            dx = dx + dy_in[0][...]
            d_ref[...] = dx
            low = dx.astype(BF16)
            dmix_out[...] = dot_tn(mixer_in_ref[...], low)
            low = dot_nt(low, mixer_ref[...]).astype(BF16)
            for i in range(4):
                outs[i][...] = dot_nn(frame_rows(peer(torus, where_ref, i)), low).astype(BF16)
        else:
            low = dx.astype(BF16)
            for i in range(4):
                outs[i][...] = dot_nn(time_rows(i), low).astype(BF16)
        wait_grads(stage, g_sem)


def attn_bwd(
    torus, space, part, where, dy, x, norms, kept, pieces, dh=None, mixing=(), dmix=None, deps=()
):
    n, width = x.shape
    last = part == 1
    rows = 192 if space or not torus else 256
    small = like(PIECE, width, dtype=BF16)
    extra = ([] if dh is None else [dh]) + list(mixing) + ([] if dmix is None else [dmix])
    out_shape = [like(16, rows, 384, dtype=BF16)]
    if not last:
        out_shape += [like(n, width)] + ([] if space else [like(n, width, dtype=BF16)])
    else:
        out_shape += [like(8, width)]
        out_shape += [like(n, width), like(width, width)] if space else []
        out_shape += [small] * 4
    return pl.pallas_call(
        functools.partial(bwd_kernel, torus, space, part, len(pieces), len(deps)),
        grid=(2,),
        out_shape=tuple(out_shape),
        in_specs=[scalars()]
        + [whole(d.shape) for d in dy]
        + [whole(x.shape), whole(norms.shape)]
        + [per_group((n, 192), 1 - part, 2)] * 4
        + [whole(e.shape) for e in extra]
        + [raw()] * (len(pieces) + len(deps)),
        out_specs=(raw(),)
        + tuple(whole(o.shape) for o in out_shape[1:]),
        scratch_shapes=attn_stores(2, width)
        + [pltpu.VMEM((n, width), BF16)] * 2
        + [pltpu.VMEM((n, 192), BF16)] * 3
        + [
            pltpu.VMEM((n, width), F32),
            pltpu.VMEM((2, 8, rows, 384), BF16),
            pltpu.SemaphoreType.DMA((2, 2)),
            pltpu.SemaphoreType.DMA((2,)),
        ],
        compiler_params=PARAMS,
        cost_estimate=cost(10**8, 10**5, 0) if space and last else cost(8 * 10**10, 12 * 10**7, 10**6),
        name=("space" if space else "time") + ("_bwd_b" if last else "_bwd_a"),
    )(where, *dy, x, norms, *kept, *extra, *pieces, *deps)


def hidden_kernel(torus, part, n_pieces, where_ref, x_ref, norms_ref, ct_ref, *refs):
    last = part == 1
    if last:
        out_in, dh_in = refs[:2]
        refs = refs[2:]
    pieces, refs = refs[:n_pieces], refs[n_pieces:]
    g_ref, out_ref, dx_ref = refs[:3]
    refs = refs[3:]
    if last:
        sums_ref, refs = refs[0], refs[1:]
    w_in, w_out, h_ref, dh_ref, stage, sems, g_sem = refs
    step = pl.program_id(0)

    @pl.when(step == 0)
    def _():
        start_loads(torus, where_ref, pieces, (w_in, w_out), sems, (0, 2) if last else (1, 3))
        x = x_ref[...]
        h_ref[...] = norm_low(normed(x)[0], norms_ref, 2)
        dh_ref[...] = dh_in[...] if last else jnp.zeros_like(dh_ref)
        out_ref[...] = out_in[...] if last else x

    wait_loads(step, (w_in, w_out), sems)
    hidden = h_ref[...]
    ct = ct_ref[...]
    up, down = w_in[step], w_out[step]
    pre = dot_nn(hidden, up)
    bell = 0.5 * (1.0 + lax.erf(pre * 0.7071067811865476))
    active = (pre * bell).astype(BF16)
    slope = bell + pre * (jnp.exp(-0.5 * pre * pre) * 0.3989422804014327)
    dpre = (dot_nn(ct, down) * slope).astype(BF16)
    out_ref[...] += dot_nt(active, down)
    dh_ref[...] += dot_nt(dpre, up)
    g_in = dot_tn(hidden, dpre).astype(BF16)
    g_out = dot_tn(ct, active).astype(BF16)
    put_grads(torus, where_ref, 1 - part, step, stage, g_ref, g_sem, g_in, g_out)

    @pl.when(step == 1)
    def _():
        dh = dh_ref[...]
        if not last:
            dx_ref[...] = dh
            wait_grads(stage, g_sem)
            return
        scaled, inverse = normed(x_ref[...])
        dx_ref[...] = ct_ref[...].astype(F32) + norm_back(dh, scaled, inverse, norms_ref[2:3])
        sums_ref[...] = norm_sums(dh, scaled)
        wait_grads(stage, g_sem)


def hidden_both(torus, part, where, x, norms, ct, pieces, before=()):
    n, width = x.shape
    last = part == 1
    out_shape = [like(16, 192, 768, dtype=BF16), like(n, width), like(n, width)]
    out_shape += [like(8, width)] if last else []
    return pl.pallas_call(
        functools.partial(hidden_kernel, torus, part, len(pieces)),
        grid=(2,),
        out_shape=tuple(out_shape),
        in_specs=[scalars(), whole(x.shape), whole(norms.shape), whole(ct.shape)]
        + [whole(b.shape) for b in before]
        + [raw()] * len(pieces),
        out_specs=(raw(),)
        + tuple(whole(o.shape) for o in out_shape[1:]),
        scratch_shapes=[
            pltpu.VMEM((2, width, 768), BF16),
            pltpu.VMEM((2, width, 768), BF16),
            pltpu.VMEM((n, width), BF16),
            pltpu.VMEM((n, width), F32),
            pltpu.VMEM((2, 8, 192, 768), BF16),
            pltpu.SemaphoreType.DMA((2, 2)),
            pltpu.SemaphoreType.DMA((2,)),
        ],
        compiler_params=PARAMS,
        cost_estimate=cost(12 * 10**10, 12 * 10**7, 2 * 10**6),
        name="hidden_b" if last else "hidden_a",
    )(where, x, norms, ct, *before, *pieces)


def mixer_kernel(n_pieces, where_ref, *refs):
    pieces, (mixer_ref, held) = refs[:n_pieces], refs[n_pieces:]
    for which in range(4):
        for lead in range(8):
            rc, ry, dp = block_at(where_ref, which, lead)
            row = pl.multiple_of(dp * 96 + (where_ref[2] ^ (ry * 2 + rc)) * 24, 8)
            rows = pieces[which][lead].astype(F32)
            held[pl.ds(row, 24), 0:384] = rows[0:24]
            held[pl.ds(row, 24), 384:768] = rows[24:48]
    mixer_ref[...] = held[...].astype(BF16)


def place_mixer(where, pieces):
    return pl.pallas_call(
        functools.partial(mixer_kernel, len(pieces)),
        grid=(1,),
        out_shape=like(768, 768, dtype=BF16),
        in_specs=[scalars()]
        + [pl.BlockSpec((p.shape[0], 48, 384), lambda i: (0, 4, 0)) for p in pieces],
        out_specs=whole((768, 768)),
        scratch_shapes=[pltpu.VMEM((768, 768), F32)],
        compiler_params=PARAMS,
        cost_estimate=cost(10**6, 3 * 10**6, 0),
        name="place_mixer",
    )(where, *pieces)


def norms_kernel(n_pieces, *refs):
    left = jnp.zeros((8, 384), F32)
    right = jnp.zeros((8, 384), F32)
    for piece in refs[:n_pieces]:
        for lead in range(piece.shape[0]):
            rows = piece[lead].astype(F32)
            left = left + rows[0:8]
            right = right + rows[8:16]
    refs[n_pieces][...] = jnp.concatenate([left, right], axis=1)


def place_norms(pieces):
    return pl.pallas_call(
        functools.partial(norms_kernel, len(pieces)),
        grid=(1,),
        out_shape=like(8, 768),
        in_specs=[pl.BlockSpec((p.shape[0], 16, 384), lambda i: (0, 12, 0)) for p in pieces],
        out_specs=whole((8, 768)),
        compiler_params=PARAMS,
        cost_estimate=cost(10**5, 10**6, 0),
        name="place_norms",
    )(*pieces)


class Order:
    def __init__(self, token):
        self.token = token

    def tie(self, *values):
        return values[0] if len(values) == 1 else values

    def go(self, value, route):
        return send(self.tie(value), route)


def after(arrived):
    return jnp.minimum(jnp.abs(arrived[(0,) * arrived.ndim].astype(F32)), 0.0)


def plus(a, b):
    return (a.astype(F32) + b.astype(F32)).astype(BF16)


class Gather:
    def __init__(self, order, shard):
        self.order, self.shard = order, shard

    def pairs(self):
        self.got = send(self.shard, SWAP_Z1)

    def second(self):
        self.pair = jnp.stack([self.shard, self.order.tie(self.got)])
        self.got = self.order.go(self.pair, SWAP_Z2)

    def sides(self, late=None):
        self.mine = jnp.concatenate([self.pair, self.order.tie(self.got)], axis=0)
        if late is not None:
            self.mine = self.mine + late.astype(BF16)
        self.got = self.order.go(self.mine, SIDE_ONE)

    def corners(self, late=None):
        self.eight = jnp.concatenate([self.mine, self.order.tie(self.got)], axis=0)
        if late is not None:
            self.eight = self.eight + late.astype(BF16)
        self.got = self.order.go(self.eight, SIDE_TWO)
        self.core_a = self.order.go(self.eight, SWAP_C)

    def cores(self, late=None):
        self.rest = self.order.tie(self.got)
        held = self.rest if late is None else self.rest + late.astype(BF16)
        self.core_b = self.order.go(held, SWAP_C)

    def done(self):
        return [self.eight, self.rest] + list(self.order.tie(self.core_a, self.core_b))


class Reduce:
    def __init__(self, order):
        self.order = order

    def cores(self, g_send):
        self.got = self.order.go(g_send, SWAP_C)

    def corners(self, g_keep, more=0.0, late=0.0):
        got = self.order.tie(self.got)

        def joined(part):
            return (g_keep[part].astype(F32) + got[part].astype(F32) + more + late).astype(BF16)

        self.sent = joined(slice(8, 16))
        late = after(self.sent)
        self.keep = joined(slice(0, 8))
        self.got = self.order.go(self.sent, SIDE_TWO)

    def sides(self, late=0.0):
        got = self.order.tie(self.got)
        self.sent = (self.keep[4:].astype(F32) + got[4:].astype(F32) + late).astype(BF16)
        self.keep = plus(self.keep[:4], got[:4])
        self.got = self.order.go(self.sent, SIDE_ONE)

    def second(self, late=0.0):
        got = self.order.tie(self.got)
        self.sent = (self.keep[2:].astype(F32) + got[2:].astype(F32) + late).astype(BF16)
        self.keep = plus(self.keep[:2], got[:2])
        self.got = self.order.go(self.sent, SWAP_Z2)

    def pairs(self):
        got = self.order.tie(self.got)
        self.sent = plus(self.keep[1], got[1])
        self.keep = self.keep[0].astype(F32) + got[0].astype(F32)
        self.got = self.order.go(self.sent, SWAP_Z1)

    def done(self):
        return self.keep + self.order.tie(self.got).astype(F32)


ROUTES = (SWAP_C, SWAP_Y, SWAP_YC)


def pack_attn(w_qkv, w_out):
    top = jnp.concatenate([w_qkv[0], w_qkv[1]], axis=1)
    low = jnp.concatenate([w_qkv[2], w_out.T], axis=1)
    return jnp.stack([top, low])


def unpack_attn(piece):
    grad_qkv = jnp.stack([piece[0, :, :192], piece[0, :, 192:], piece[1, :, :192]])
    return grad_qkv, piece[1, :, 192:].T


def full_gather(packed):
    return lax.all_gather(lax.all_gather(packed, "dp", axis=1, tiled=True), "tensor", axis=0)


def full_reduce(g_keep, g_send):
    rows, lanes = g_keep.shape[1:]
    full = jnp.stack([g_keep[:8], g_send[:8], g_keep[8:], g_send[8:]]).reshape(4, 8, 2, rows // 2, lanes)
    full = full.transpose(0, 2, 1, 3, 4).reshape(4, 2, 4 * rows, lanes).astype(F32)
    mine = lax.psum_scatter(full, "tensor", scatter_dimension=0, tiled=False)
    return lax.psum_scatter(mine, "dp", scatter_dimension=1, tiled=True)


def swap_all(pieces):
    got = lax.all_to_all(jnp.stack(pieces), "tensor", 0, 0, tiled=True)
    return [got[i] for i in range(4)]


def reorder(torus, groups, t):
    if not torus:
        return groups
    swap_c = (t & 1) == 1
    swap_y = (t >> 1) == 1
    groups = jnp.where(swap_c, jnp.stack([groups[1], groups[0], groups[3], groups[2]]), groups)
    return jnp.where(swap_y, jnp.stack([groups[2], groups[3], groups[0], groups[1]]), groups)


def padded(frames):
    return jnp.pad(frames, ((0, 0), (0, PAD - PATCHES), (0, 0))).reshape(2 * PAD, -1)


def trimmed(rows):
    return rows.reshape(2, PAD, -1)[:, :PATCHES]


def to_frames(torus, pieces, t):
    groups = reorder(torus, jnp.stack([p[:98].reshape(2, 49, -1) for p in pieces]), t)
    return groups.transpose(1, 0, 2, 3).reshape(2, PATCHES, -1)


def shards(
    torus,
    clip_tokens,
    time_qkv,
    time_out,
    time_mixer,
    space_qkv,
    space_out,
    hidden_in,
    hidden_out,
    norm_gain,
    norm_bias,
    cotangent,
):
    dp = lax.axis_index("dp")
    t = lax.axis_index("tensor")
    z, x = dp >> 1, dp & 1
    where = jnp.stack([z, x, t, t]).astype(jnp.int32)
    width = clip_tokens.shape[-1]
    tokens = clip_tokens[0].reshape(2, PATCHES, width)
    norm_rows = jnp.concatenate([norm_gain, norm_bias], axis=0)
    share = norm_rows.shape[1]
    order = Order(where)

    def by_patch_of(got):
        return jnp.stack(got).transpose(2, 0, 1, 3).reshape(392, width)

    time_w = pack_attn(time_qkv, time_out)
    groups = reorder(torus, tokens.reshape(2, 4, 49, width).transpose(1, 0, 2, 3), t)
    if torus:
        spread = lax.dynamic_update_slice(
            jnp.zeros((8, width), BF16), norm_rows, (0, (dp * 4 + t) * share)
        )
        timed = Gather(
            order,
            jnp.concatenate([time_w.reshape(192, 384), spread[:, :384], spread[:, 384:]], axis=0),
        )
        timed.pairs()
        moved = [order.go(groups[i + 1], ROUTES[i]) for i in range(3)]
        space_w = pack_attn(space_qkv, space_out)
        spaced = Gather(
            order,
            jnp.concatenate(
                [space_w.reshape(192, 384), time_mixer[:, :384], time_mixer[:, 384:]], axis=0
            ),
        )
        spaced.pairs()
        ff = Gather(order, jnp.concatenate([hidden_in, hidden_out.T], axis=0))
        ff.pairs()
        timed.second()
        spaced.second()
        by_patch = by_patch_of([groups[0]] + list(order.tie(*moved)))
        timed.sides(after(by_patch) + after(ff.got))
        ff.second()
        base = order.tie(padded(tokens))
        ct = order.tie(padded(cotangent[0].reshape(2, PATCHES, width)))
        timed.corners(after(spaced.got) + after(base) + after(ct))
        spaced.sides()
        timed.cores()
        spaced.corners()
        ff.sides()
        time_p = timed.done()
        norms = place_norms(time_p)
    else:
        space_w = pack_attn(space_qkv, space_out)
        by_patch = by_patch_of(swap_all([groups[i] for i in range(4)]))
        ct = padded(cotangent[0].reshape(2, PATCHES, width))
        base = padded(tokens)
        time_p = [full_gather(time_w)]
        space_p = [full_gather(space_w)]
        ff_p = [full_gather(jnp.stack([hidden_in, hidden_out.T]))]
        mixer = lax.all_gather(time_mixer, AXES, axis=0, tiled=True)
        norms = lax.all_gather(norm_rows, AXES, axis=1, tiled=True).astype(F32)
        norms = jnp.pad(norms, ((0, 2), (0, 0)))

    def trade(pieces):
        if not torus:
            return swap_all(pieces)
        return [pieces[0]] + [order.go(pieces[i + 1], ROUTES[i]) for i in range(3)]

    by_patch = order.tie(by_patch)
    y_pieces, kept_time, high_time = time_fwd(
        torus, where, by_patch, norms, time_p, [ff.mine] if torus else []
    )
    y_pieces = trade(list(order.tie(*y_pieces)))
    if torus:
        spaced.cores()
        space_p = spaced.done()
        mixer = place_mixer(where, space_p)
    deps = []
    if torus:
        ff.corners(after(y_pieces[2]) + after(y_pieces[3]))
        deps = [ff.eight]
    x2, x1, mixer_in, kept_space, high_space = space_fwd(
        torus, where, base, norms, mixer, y_pieces, space_p, deps
    )
    if torus:
        ff.cores(after(x2))
        ff_p = ff.done()
    highs = jnp.stack([high_time[:, :3, 0], high_space[:, :3, 0]], axis=1)
    if torus:
        spots = reorder(torus, highs, t).reshape(1, 24)
        upper = lax.reduce_precision(spots, 8, 7)
        spots = jnp.concatenate([upper, spots - upper], axis=0)
        high_rows = lax.dynamic_update_slice(
            jnp.zeros((2, width), F32), spots, (0, (dp * 4 + t) * 24)
        )
    g1_ff, *before = hidden_both(torus, 0, where, x2, norms, ct, half(torus, ff_p, 1))
    if torus:
        red_ff, red_space, red_time = Reduce(order), Reduce(order), Reduce(order)
        red_ff.cores(g1_ff)
    g0_ff, out_rows, d_space, sums_three = hidden_both(
        torus, 1, where, x2, norms, ct, half(torus, ff_p, 0), tuple(before)
    )
    deps = []
    if torus:
        red_ff.corners(g0_ff)
        deps = [red_ff.sent]
    d_space = order.tie(d_space)
    g1_space, dh = attn_bwd(
        torus, True, 0, where, [d_space], x1, norms, kept_space, half(torus, space_p, 1), deps=deps
    )
    g1_space, dh = order.tie(g1_space, dh)
    if torus:
        red_space.cores(g1_space)
        deps = []
    dh = order.tie(dh)
    g0_space, sums_two, d_time, dmix, *dy = attn_bwd(
        torus,
        True,
        1,
        where,
        [d_space],
        x1,
        norms,
        kept_space,
        half(torus, space_p, 0),
        dh,
        (mixer_in, mixer),
        deps=deps,
    )
    g0_space, *dy = order.tie(g0_space, *dy)
    dy = trade(dy)
    if torus:
        arrived = after(dy[2]) + after(dy[3])
        red_ff.sides(arrived)
        deps = [red_ff.sent]
    dy = list(order.tie(*dy))
    g1_time, dh, dy = attn_bwd(
        torus,
        False,
        0,
        where,
        dy,
        by_patch,
        norms,
        kept_time,
        half(torus, time_p, 1),
        dmix=dmix,
        deps=deps,
    )
    g1_time, dh, dy = order.tie(g1_time, dh, dy)
    if torus:
        red_time.cores(g1_time)
        red_space.corners(g0_space, late=after(dh))
        red_ff.second()
        deps = [red_ff.sent, red_space.sent]
    dh = order.tie(dh)
    g0_time, sums_one, *dx = attn_bwd(
        torus,
        False,
        1,
        where,
        [dy],
        by_patch,
        norms,
        kept_time,
        half(torus, time_p, 0),
        dh,
        dmix=dmix,
        deps=deps,
    )
    g0_time, sums_one, *dx = order.tie(g0_time, sums_one, *dx)

    sums = jnp.concatenate(
        [sums_one[:1], sums_two[:1], sums_three[:1], sums_one[1:2], sums_two[1:2], sums_three[1:2]]
    )
    if torus:
        sums = jnp.concatenate([sums, high_rows], axis=0)
        sums = sums + send(sums, SWAP_C)
        more = jnp.concatenate([sums[:, :384], sums[:, 384:]], axis=0)
        red_space.sides()
        red_time.corners(g0_time, jnp.pad(more, ((240, 0), (0, 0))), after(red_space.sent))
        dx = trade(dx)
        red_time.sides()
        late = after(red_time.sent)
        red_space.second(late)
        late = late.astype(BF16)
        input_grad = trimmed(d_time) + to_frames(torus, [d + late for d in dx], t).astype(F32)
        red_time.second()
        red_space.pairs()
        red_ff.pairs()
        space_piece = red_space.done().reshape(2, 96, 384)
        ff_piece = red_ff.done().reshape(2, 96, 768)
        red_time.pairs()
        piece = red_time.done()
        mixer_grad = jnp.concatenate([piece[192:216], piece[216:240]], axis=1)
        time_piece = piece[:192].reshape(2, 96, 384)
        total = jnp.concatenate([piece[240:248], piece[248:256]], axis=1)
        mine = lax.dynamic_slice(total, (0, (dp * 4 + t) * share), (6, share))
        highest = jnp.max((total[6] + total[7]).reshape(32, 4, 2, 3), axis=0)
        highest = lax.dynamic_index_in_dim(highest, t, 0, keepdims=False)
    else:
        ff_piece = full_reduce(g0_ff, g1_ff)
        space_piece = full_reduce(g0_space, g1_space)
        time_piece = full_reduce(g0_time, g1_time)
        mixer_grad = lax.psum_scatter(dmix, AXES, scatter_dimension=0, tiled=True)
        input_grad = trimmed(d_time) + to_frames(torus, swap_all(dx), t).astype(F32)
        highest = lax.dynamic_index_in_dim(lax.pmax(highs, AXES), t, 0, keepdims=False)
        mine = lax.psum_scatter(sums, AXES, scatter_dimension=1, tiled=True)
    qk_clip = jnp.sqrt(TAU / jnp.maximum(highest, TAU))
    time_qkv_grad, time_out_grad = unpack_attn(time_piece)
    space_qkv_grad, space_out_grad = unpack_attn(space_piece)
    return (
        trimmed(out_rows).reshape(1, 392, width),
        input_grad.reshape(1, 392, width),
        time_qkv_grad,
        time_out_grad,
        mixer_grad,
        space_qkv_grad,
        space_out_grad,
        ff_piece[0],
        ff_piece[1].T,
        mine[:3],
        mine[3:],
        qk_clip,
    )


def solution(mesh):
    sizes = dict(mesh.shape)
    torus = sizes["dp"] == 8 and sizes["tensor"] == 4
    in_specs = (
        P("dp", "tensor", None),
        P(None, "dp", "tensor"),
        P("tensor", "dp"),
        P(("dp", "tensor"), None),
        P(None, "dp", "tensor"),
        P("tensor", "dp"),
        P("dp", "tensor"),
        P("tensor", "dp"),
        P(None, ("dp", "tensor")),
        P(None, ("dp", "tensor")),
        P("dp", "tensor", None),
    )
    out_specs = (
        P("dp", "tensor", None),
        P("dp", "tensor", None),
        P(None, "dp", "tensor"),
        P("tensor", "dp"),
        P(("dp", "tensor"), None),
        P(None, "dp", "tensor"),
        P("tensor", "dp"),
        P("dp", "tensor"),
        P("tensor", "dp"),
        P(None, ("dp", "tensor")),
        P(None, ("dp", "tensor")),
        P(None, "tensor"),
    )
    body = functools.partial(shards, torus)
    return jax.shard_map(body, mesh=mesh, in_specs=in_specs, out_specs=out_specs, check_vma=False)
```

```python
import functools

import jax
import jax.numpy as jnp
from jax import lax
from jax.experimental import pallas as pl
from jax.experimental.pallas import tpu as pltpu
from jax.sharding import PartitionSpec as P

HD = 64
FRAMES = 8
PATCHES = 196
PAD = 208
SCALE = 0.125
TAU = 2.0
EPS = 1e-06
AXES = ("dp", "tensor")
F32 = jnp.float32
BF16 = jnp.bfloat16
PIECE = 112
VMEM_LIMIT = 60 * 1024 * 1024


def place(z, x, y, c):
    return ((z * 2 + x) * 2 + y) * 2 + c


ALL = [(z, x, y, c) for z in range(4) for x in range(2) for y in range(2) for c in range(2)]


def pairs(move, keep=lambda z, x, y, c: True):
    return [(place(*i), place(*move(*i))) for i in ALL if keep(*i)]


SWAP_C = pairs(lambda z, x, y, c: (z, x, y, 1 - c))
SWAP_Y = pairs(lambda z, x, y, c: (z, x, 1 - y, c))
SWAP_YC = pairs(lambda z, x, y, c: (z, x, 1 - y, 1 - c))
SWAP_X = pairs(lambda z, x, y, c: (z, 1 - x, y, c))
SWAP_Z1 = pairs(lambda z, x, y, c: (z ^ 1, x, y, c))
SWAP_Z2 = pairs(lambda z, x, y, c: (z ^ 2, x, y, c))
SIDE_ONE = pairs(lambda z, x, y, c: (z, x, 1 - y, c) if c else (z, 1 - x, y, c))
SIDE_TWO = pairs(lambda z, x, y, c: (z, 1 - x, y, c) if c else (z, x, 1 - y, c))


def send(value, route):
    return lax.ppermute(value, AXES, route)


def dot_nn(a, b):
    return lax.dot_general(a, b, (((1,), (0,)), ((), ())), preferred_element_type=F32)


def dot_nt(a, b):
    return lax.dot_general(a, b, (((1,), (1,)), ((), ())), preferred_element_type=F32)


def dot_tn(a, b):
    return lax.dot_general(a, b, (((0,), (0,)), ((), ())), preferred_element_type=F32)


def blocks_in(pieces):
    found, rc, block = [], 0, 0
    for which, piece in enumerate(pieces):
        for lead in range(piece.shape[0]):
            found.append((which, lead, rc, block, lead % 4))
            if lead % 4 == 3:
                block += 1
        if block == 4:
            rc, block = rc + 1, 0
    return found


def block_at(where_ref, rc, block, slot):
    low, high = block & 1, block >> 1
    first = ((where_ref[2] ^ rc) & 1) == 0
    rx = jnp.where(first, low, high)
    ry = jnp.where(first, high, low)
    return ry, (where_ref[0] ^ slot) * 2 + (where_ref[1] ^ rx)


def start_loads(torus, where_ref, pieces, stores, sems, groups):
    if not torus:
        for i, r in enumerate(groups):
            for b in range(2):
                pltpu.make_async_copy(pieces[0].at[r, b], stores[b].at[i], sems.at[i, b]).start()
        return
    every = len(groups) == 4
    for which, lead, rc, block, slot in blocks_in(pieces):
        ry, dp = block_at(where_ref, rc if every else groups[0], block, slot)
        i = ry * 2 + rc if every else ry
        row = pl.multiple_of(dp * 96, 96)
        for b in range(2):
            pltpu.make_async_copy(
                pieces[which].at[lead, pl.ds(b * 96, 96), :],
                stores[b].at[i, pl.ds(row, 96), :],
                sems.at[i, b],
            ).start()


def wait_loads(i, stores, sems):
    for b in range(2):
        pltpu.make_async_copy(stores[b].at[i], stores[b].at[i], sems.at[i, b]).wait()


def out_block(torus, where_ref, rc, step, dp):
    if not torus:
        return step * 8 + dp
    slot = where_ref[0] ^ (dp // 2)
    rx, ry = where_ref[1] ^ (dp % 2), step
    first = ((where_ref[2] ^ rc) & 1) == 0
    return jnp.where(first, ry, rx) * 8 + jnp.where(first, rx, ry) * 4 + slot


def peer(torus, where_ref, r):
    return where_ref[2] ^ r if torus else r


def put_grads(torus, where_ref, rc, step, stage, g_ref, sem, first, second, third=None):
    for dp in range(8):
        stage[step, dp, 0:96, :] = first[dp * 96 : (dp + 1) * 96]
        stage[step, dp, 96:192, :] = second[dp * 96 : (dp + 1) * 96]
        if third is not None:
            stage[step, dp, 192:, :] = third[dp]
        block = out_block(torus, where_ref, rc, step, dp)
        pltpu.make_async_copy(stage.at[step, dp], g_ref.at[block], sem.at[step]).start()


def wait_grads(stage, sem):
    for i in range(2):
        pltpu.make_async_copy(stage.at[i], stage.at[i], sem.at[i]).wait()


def normed(rows):
    mean = jnp.mean(rows, axis=-1, keepdims=True)
    centered = rows - mean
    inverse = lax.rsqrt(jnp.mean(centered * centered, axis=-1, keepdims=True) + EPS)
    return centered * inverse, inverse


def norm_low(scaled, norms_ref, norm):
    return (scaled * norms_ref[norm : norm + 1] + norms_ref[3 + norm : 4 + norm]).astype(BF16)


def norm_back(dh, scaled, inverse, gain):
    weighted = dh * gain
    return inverse * (
        weighted
        - jnp.mean(weighted, axis=-1, keepdims=True)
        - scaled * jnp.mean(weighted * scaled, axis=-1, keepdims=True)
    )


def norm_sums(dh, scaled, norm):
    gain = jnp.sum(dh * scaled, axis=0, keepdims=True)
    bias = jnp.sum(dh, axis=0, keepdims=True)
    row = lax.broadcasted_iota(jnp.int32, (8, dh.shape[1]), 0)
    return jnp.where(row == norm, gain, jnp.where(row == 3 + norm, bias, 0.0))


def ones_at(chosen):
    return jnp.where(chosen, 1.0, 0.0).astype(BF16)


def time_rows(r):
    row = lax.broadcasted_iota(jnp.int32, (PIECE, 392), 0)
    col = lax.broadcasted_iota(jnp.int32, (PIECE, 392), 1)
    return ones_at((((col >> 1) & 3) == r) & (row == (col & 1) * 49 + (col >> 3)))


def frame_rows(group):
    row = lax.broadcasted_iota(jnp.int32, (PIECE, 2 * PAD), 0)
    col = lax.broadcasted_iota(jnp.int32, (PIECE, 2 * PAD), 1)
    second = jnp.where(col >= PAD, 1, 0)
    patch = col - second * PAD - group * 49
    return ones_at((patch >= 0) & (patch < 49) & (row == second * 49 + patch))


def blocks_of(space):
    return ((0, PAD), (PAD, PAD)) if space else ((0, 192), (192, 200))


def keep_mask(space, size):
    row = lax.broadcasted_iota(jnp.int32, (size, size), 0)
    col = lax.broadcasted_iota(jnp.int32, (size, size), 1)
    if space:
        return row < PATCHES
    return (row >> 3) == (col >> 3)


def head_lanes(size):
    lane = lax.broadcasted_iota(jnp.int32, (size, 192), 1)
    return [(lane >= j * HD) & (lane < (j + 1) * HD) for j in range(3)]


def whole(shape):
    return pl.BlockSpec(shape, lambda i: (0,) * len(shape))


def raw():
    return pl.BlockSpec(memory_space=pl.ANY)


def scalars():
    return pl.BlockSpec(memory_space=pltpu.SMEM)


def like(*shape, dtype=F32):
    return jax.ShapeDtypeStruct(shape, dtype)


def cost(flops, size, exps):
    return pl.CostEstimate(flops=flops, bytes_accessed=size, transcendentals=exps)


PARAMS = pltpu.CompilerParams(vmem_limit_bytes=VMEM_LIMIT)


def heads_fwd(space, hidden, w_qk, w_vo, q_ref, k_ref, v_ref, o_ref, high_ref):
    qk = dot_nn(hidden, w_qk)
    q_ref[0] = qk[:, :192].astype(BF16)
    k_ref[0] = qk[:, 192:].astype(BF16)
    v_ref[0] = dot_nn(hidden, w_vo[:, :192]).astype(BF16)
    tops = [None, None, None]
    for start, size in blocks_of(space):
        q = q_ref[0, pl.ds(start, size), :]
        k = k_ref[0, pl.ds(start, size), :]
        v = v_ref[0, pl.ds(start, size), :]
        keep = keep_mask(space, size)
        zero = jnp.zeros_like(q)
        q = q * jnp.asarray(SCALE, BF16)
        mixed = None
        for j, mine in enumerate(head_lanes(size)):
            logits = jnp.where(keep, dot_nt(k, jnp.where(mine, q, zero)), -1e30)
            peak = jnp.max(logits, axis=0, keepdims=True)
            exponent = jnp.exp(logits - peak)
            weights = (exponent * (1.0 / jnp.sum(exponent, axis=0, keepdims=True))).astype(BF16)
            part = dot_tn(weights, jnp.where(mine, v, zero))
            mixed = part if mixed is None else mixed + part
            if space:
                col = lax.broadcasted_iota(jnp.int32, (1, size), 1)
                peak = jnp.where(col < PATCHES, peak, -1e30)
            top = jnp.max(peak, axis=1, keepdims=True)
            tops[j] = top if tops[j] is None else jnp.maximum(tops[j], top)
        o_ref[0, pl.ds(start, size), :] = mixed.astype(BF16)
    row8 = lax.broadcasted_iota(jnp.int32, (8, 128), 0)
    high = jnp.full((8, 128), -1e30, F32)
    for j in range(3):
        high = jnp.where(row8 == j, jnp.broadcast_to(tops[j], (8, 128)), high)
    high_ref[0] = high
    return dot_nt(o_ref[0], w_vo[:, 192:])


def time_fwd_kernel(torus, n_pieces, n_deps, where_ref, x_ref, norms_ref, *refs):
    pieces, refs = refs[:n_pieces], refs[n_pieces + n_deps :]
    outs, saved, refs = refs[:4], refs[4:9], refs[9:]
    w_qk, w_vo, h_ref, y_ref, sems = refs
    r = pl.program_id(0)

    @pl.when(r == 0)
    def _():
        start_loads(torus, where_ref, pieces, (w_qk, w_vo), sems, range(4))
        h_ref[...] = norm_low(normed(x_ref[...].astype(F32))[0], norms_ref, 0)
        y_ref[...] = jnp.zeros_like(y_ref)

    wait_loads(r, (w_qk, w_vo), sems)
    y_ref[...] += heads_fwd(False, h_ref[...], w_qk[r], w_vo[r], *saved)

    @pl.when(r == 3)
    def _():
        low = y_ref[...].astype(BF16)
        for i in range(4):
            outs[i][...] = dot_nn(time_rows(i), low).astype(BF16)


def space_fwd_kernel(torus, n_pieces, n_deps, where_ref, base_ref, norms_ref, mixer_ref, y0, y1, y2, y3, *refs):
    pieces, refs = refs[:n_pieces], refs[n_pieces + n_deps :]
    x2_ref, x1_ref, mixer_in_ref = refs[:3]
    saved, refs = refs[3:8], refs[8:]
    w_qk, w_vo, h_ref, sems = refs
    r = pl.program_id(0)

    @pl.when(r == 0)
    def _():
        start_loads(torus, where_ref, pieces, (w_qk, w_vo), sems, range(4))
        placed = None
        for i, piece in enumerate((y0, y1, y2, y3)):
            part = dot_tn(frame_rows(peer(torus, where_ref, i)), piece[...])
            placed = part if placed is None else placed + part
        mixer_in = placed.astype(BF16)
        mixer_in_ref[...] = mixer_in
        x1 = base_ref[...].astype(F32) + dot_nn(mixer_in, mixer_ref[...])
        x1_ref[...] = x1
        x2_ref[...] = x1
        h_ref[...] = norm_low(normed(x1)[0], norms_ref, 1)

    wait_loads(r, (w_qk, w_vo), sems)
    x2_ref[...] += heads_fwd(True, h_ref[...], w_qk[r], w_vo[r], *saved)


def per_group(shape, first=0, step=1):
    return pl.BlockSpec((1,) + shape, lambda i: (first + step * i,) + (0,) * len(shape))


def kept_shapes(n):
    return (like(4, n, 192, dtype=BF16),) * 4 + (like(4, 8, 128),)


def kept_specs(n):
    return (per_group((n, 192)),) * 4 + (per_group((8, 128)),)


def half(torus, pieces, rc):
    n = len(pieces) // 2
    return pieces[n * rc : n * rc + n] if torus else pieces


def attn_stores(groups, width):
    return [
        pltpu.VMEM((groups, width, 384), BF16),
        pltpu.VMEM((groups, width, 384), BF16),
    ]


def time_fwd(torus, where, x, norms, pieces, deps):
    n, width = x.shape
    outs = pl.pallas_call(
        functools.partial(time_fwd_kernel, torus, len(pieces), len(deps)),
        grid=(4,),
        out_shape=(like(PIECE, width, dtype=BF16),) * 4 + kept_shapes(n),
        in_specs=[scalars(), whole(x.shape), whole(norms.shape)]
        + [raw()] * (len(pieces) + len(deps)),
        out_specs=(whole((PIECE, width)),) * 4 + kept_specs(n),
        scratch_shapes=attn_stores(4, width)
        + [
            pltpu.VMEM((n, width), BF16),
            pltpu.VMEM((n, width), F32),
            pltpu.SemaphoreType.DMA((4, 2)),
        ],
        compiler_params=PARAMS,
        cost_estimate=cost(3 * 10**9, 12 * 10**6, 10**6),
        name="time_fwd",
    )(where, x, norms, *pieces, *deps)
    return list(outs[:4]), list(outs[4:8]), outs[8]


def space_fwd(torus, where, base, norms, mixer, y_pieces, pieces, deps):
    n, width = base.shape
    outs = pl.pallas_call(
        functools.partial(space_fwd_kernel, torus, len(pieces), len(deps)),
        grid=(4,),
        out_shape=(like(n, width), like(n, width), like(n, width, dtype=BF16)) + kept_shapes(n),
        in_specs=[scalars(), whole(base.shape), whole(norms.shape), whole(mixer.shape)]
        + [whole((PIECE, width))] * 4
        + [raw()] * (len(pieces) + len(deps)),
        out_specs=(whole((n, width)),) * 3 + kept_specs(n),
        scratch_shapes=attn_stores(4, width)
        + [pltpu.VMEM((n, width), BF16), pltpu.SemaphoreType.DMA((4, 2))],
        compiler_params=PARAMS,
        cost_estimate=cost(3 * 10**9, 12 * 10**6, 10**6),
        name="space_fwd",
    )(where, base, norms, mixer, *y_pieces, *pieces, *deps)
    return outs[0], outs[1], outs[2], list(outs[3:7]), outs[7]


def heads_bwd(space, dy, hidden, w_qk, w_vo, q_ref, k_ref, v_ref, o_ref, dq_ref, dk_ref, dv_ref):
    dv_ref[...] = dot_nn(dy, w_vo)[:, 192:].astype(BF16)
    for start, size in blocks_of(space):
        q = q_ref[0, pl.ds(start, size), :]
        k = k_ref[0, pl.ds(start, size), :]
        v = v_ref[0, pl.ds(start, size), :]
        do = dv_ref[pl.ds(start, size), :]
        keep = keep_mask(space, size)
        zero = jnp.zeros_like(q)
        q = q * jnp.asarray(SCALE, BF16)
        dq = dk = dv = None
        for mine in head_lanes(size):
            q_j = jnp.where(mine, q, zero)
            do_j = jnp.where(mine, do, zero)
            logits = jnp.where(keep, dot_nt(k, q_j), -1e30)
            exponent = jnp.exp(logits - jnp.max(logits, axis=0, keepdims=True))
            weights = exponent * (1.0 / jnp.sum(exponent, axis=0, keepdims=True))
            dweights = dot_nt(v, do_j)
            inner = jnp.sum(dweights * weights, axis=0, keepdims=True)
            dlogits = (weights * (dweights - inner)).astype(BF16)
            dv_j = dot_nn(weights.astype(BF16), do_j)
            dk_j = dot_nn(dlogits, q_j)
            dq_j = dot_tn(dlogits, jnp.where(mine, k, zero))
            dq = dq_j if dq is None else dq + dq_j
            dk = dk_j if dk is None else dk + dk_j
            dv = dv_j if dv is None else dv + dv_j
        dq_ref[pl.ds(start, size), :] = (dq * SCALE).astype(BF16)
        dk_ref[pl.ds(start, size), :] = dk.astype(BF16)
        dv_ref[pl.ds(start, size), :] = dv.astype(BF16)
    dqk = jnp.concatenate([dq_ref[...], dk_ref[...]], axis=1)
    dv = dv_ref[...]
    dh = dot_nt(dqk, w_qk) + dot_nt(dv, w_vo[:, :192])
    g_qk = dot_tn(hidden, dqk).astype(BF16)
    g_vo = jnp.concatenate([dot_tn(hidden, dv), dot_tn(dy, o_ref[0])], axis=1).astype(BF16)
    return dh, g_qk, g_vo


def bwd_kernel(torus, space, part, n_pieces, n_deps, n_through, where_ref, *refs):
    norm = 1 if space else 0
    last = part == 1
    n_dy = 1 if space or last else 4
    dy_in, refs = refs[:n_dy], refs[n_dy:]
    x_ref, norms_ref = refs[:2]
    kept, refs = refs[2:6], refs[6:]
    if last:
        dh_in, refs = refs[0], refs[1:]
    if space and last:
        mixer_in_ref, mixer_ref = refs[:2]
        refs = refs[2:]
    if not space:
        dmix_ref, refs = refs[0], refs[1:]
    pieces, refs = refs[:n_pieces], refs[n_pieces + n_deps + n_through :]
    g_ref, refs = refs[0], refs[1:]
    if not last:
        dh_out, refs = refs[0], refs[1:]
        if not space:
            dy_out, refs = refs[0], refs[1:]
    else:
        sums_ref, refs = refs[0], refs[1:]
        if space:
            d_ref, dmix_out = refs[:2]
            refs = refs[2:]
        outs, refs = refs[:4], refs[4:]
    w_qk, w_vo, h_ref, dy_ref, dq_ref, dk_ref, dv_ref, dh_ref, stage, sems, g_sem = refs[n_through:]
    step = pl.program_id(0)
    r = 2 * step + (1 - part)

    @pl.when(step == 0)
    def _():
        start_loads(torus, where_ref, pieces, (w_qk, w_vo), sems, (0, 2) if last else (1, 3))
        h_ref[...] = norm_low(normed(x_ref[...].astype(F32))[0], norms_ref, norm)
        if n_dy == 1:
            dy_ref[...] = dy_in[0][...].astype(BF16)
        else:
            placed = None
            for i in range(4):
                term = dot_tn(time_rows(i), dy_in[i][...])
                placed = term if placed is None else placed + term
            dy_ref[...] = placed.astype(BF16)
            dy_out[...] = placed.astype(BF16)
        dh_ref[...] = dh_in[...] if last else jnp.zeros_like(dh_ref)

    wait_loads(step, (w_qk, w_vo), sems)
    dh, g_qk, g_vo = heads_bwd(
        space, dy_ref[...], h_ref[...], w_qk[step], w_vo[step], *kept, dq_ref, dk_ref, dv_ref
    )
    dh_ref[...] += dh
    third = None
    if not space and torus:
        t = where_ref[2] ^ r
        third = []
        for dp in range(8):
            block = dmix_ref[pl.ds(pl.multiple_of(dp * 96 + t * 24, 8), 24), :]
            block = jnp.concatenate([block[:, :384], block[:, 384:], jnp.zeros((16, 384), F32)], axis=0)
            third.append(block.astype(BF16))
    put_grads(torus, where_ref, 1 - part, step, stage, g_ref, g_sem, g_qk, g_vo, third)

    @pl.when(step == 1)
    def _():
        if not last:
            dh_out[...] = dh_ref[...]
            wait_grads(stage, g_sem)
            return
        scaled, inverse = normed(x_ref[...].astype(F32))
        total = dh_ref[...]
        sums_ref[...] = norm_sums(total, scaled, norm)
        dx = norm_back(total, scaled, inverse, norms_ref[norm : norm + 1])
        if space:
            dx = dx + dy_in[0][...]
            d_ref[...] = dx
            low = dx.astype(BF16)
            dmix_out[...] = dot_tn(mixer_in_ref[...], low)
            low = dot_nt(low, mixer_ref[...]).astype(BF16)
            for i in range(4):
                outs[i][...] = dot_nn(frame_rows(peer(torus, where_ref, i)), low).astype(BF16)
        else:
            low = dx.astype(BF16)
            for i in range(4):
                outs[i][...] = dot_nn(time_rows(i), low).astype(BF16)
        wait_grads(stage, g_sem)


def attn_bwd(
    torus,
    space,
    part,
    where,
    dy,
    x,
    norms,
    kept,
    pieces,
    dh=None,
    mixing=(),
    dmix=None,
    deps=(),
    through=(),
):
    n, width = x.shape
    last = part == 1
    rows = 192 if space or not torus else 256
    small = like(PIECE, width, dtype=BF16)
    extra = ([] if dh is None else [dh]) + list(mixing) + ([] if dmix is None else [dmix])
    first = 1 + len(dy) + 2 + len(kept) + len(extra) + len(pieces) + len(deps)
    out_shape = [like(16, rows, 384, dtype=BF16)]
    if not last:
        out_shape += [like(n, width)] + ([] if space else [like(n, width, dtype=BF16)])
    else:
        out_shape += [like(8, width)]
        out_shape += [like(n, width), like(width, width)] if space else []
        out_shape += [small] * 4
    return pl.pallas_call(
        functools.partial(
            bwd_kernel, torus, space, part, len(pieces), len(deps), len(through)
        ),
        grid=(2,),
        out_shape=tuple(out_shape) + tuple(like(*v.shape, dtype=v.dtype) for v in through),
        in_specs=[scalars()]
        + [whole(d.shape) for d in dy]
        + [whole(x.shape), whole(norms.shape)]
        + [per_group((n, 192), 1 - part, 2)] * 4
        + [whole(e.shape) for e in extra]
        + [raw()] * (len(pieces) + len(deps) + len(through)),
        out_specs=(raw(),)
        + tuple(whole(o.shape) for o in out_shape[1:])
        + (raw(),) * len(through),
        input_output_aliases={first + i: len(out_shape) + i for i in range(len(through))},
        scratch_shapes=attn_stores(2, width)
        + [pltpu.VMEM((n, width), BF16)] * 2
        + [pltpu.VMEM((n, 192), BF16)] * 3
        + [
            pltpu.VMEM((n, width), F32),
            pltpu.VMEM((2, 8, rows, 384), BF16),
            pltpu.SemaphoreType.DMA((2, 2)),
            pltpu.SemaphoreType.DMA((2,)),
        ],
        compiler_params=PARAMS,
        cost_estimate=cost(10**8, 10**5, 0) if space and last else cost(8 * 10**10, 12 * 10**7, 10**6),
        name=("space" if space else "time") + ("_bwd_b" if last else "_bwd_a"),
    )(where, *dy, x, norms, *kept, *extra, *pieces, *deps, *through)


def hidden_kernel(torus, part, n_pieces, where_ref, x_ref, norms_ref, ct_ref, *refs):
    last = part == 1
    if last:
        out_in, dh_in = refs[:2]
        refs = refs[2:]
    pieces, refs = refs[:n_pieces], refs[n_pieces:]
    g_ref, out_ref, dx_ref = refs[:3]
    refs = refs[3:]
    if last:
        sums_ref, refs = refs[0], refs[1:]
    w_in, w_out, h_ref, dh_ref, stage, sems, g_sem = refs
    step = pl.program_id(0)

    @pl.when(step == 0)
    def _():
        start_loads(torus, where_ref, pieces, (w_in, w_out), sems, (0, 2) if last else (1, 3))
        x = x_ref[...]
        h_ref[...] = norm_low(normed(x)[0], norms_ref, 2)
        dh_ref[...] = dh_in[...] if last else jnp.zeros_like(dh_ref)
        out_ref[...] = out_in[...] if last else x

    wait_loads(step, (w_in, w_out), sems)
    hidden = h_ref[...]
    ct = ct_ref[...]
    up, down = w_in[step], w_out[step]
    pre = dot_nn(hidden, up)
    bell = 0.5 * (1.0 + lax.erf(pre * 0.7071067811865476))
    active = (pre * bell).astype(BF16)
    slope = bell + pre * (jnp.exp(-0.5 * pre * pre) * 0.3989422804014327)
    dpre = (dot_nn(ct, down) * slope).astype(BF16)
    out_ref[...] += dot_nt(active, down)
    dh_ref[...] += dot_nt(dpre, up)
    g_in = dot_tn(hidden, dpre).astype(BF16)
    g_out = dot_tn(ct, active).astype(BF16)
    put_grads(torus, where_ref, 1 - part, step, stage, g_ref, g_sem, g_in, g_out)

    @pl.when(step == 1)
    def _():
        dh = dh_ref[...]
        if not last:
            dx_ref[...] = dh
            wait_grads(stage, g_sem)
            return
        scaled, inverse = normed(x_ref[...])
        dx_ref[...] = ct_ref[...].astype(F32) + norm_back(dh, scaled, inverse, norms_ref[2:3])
        sums_ref[...] = norm_sums(dh, scaled, 2)
        wait_grads(stage, g_sem)


def hidden_both(torus, part, where, x, norms, ct, pieces, before=()):
    n, width = x.shape
    last = part == 1
    out_shape = [like(16, 192, 768, dtype=BF16), like(n, width), like(n, width)]
    out_shape += [like(8, width)] if last else []
    return pl.pallas_call(
        functools.partial(hidden_kernel, torus, part, len(pieces)),
        grid=(2,),
        out_shape=tuple(out_shape),
        in_specs=[scalars(), whole(x.shape), whole(norms.shape), whole(ct.shape)]
        + [whole(b.shape) for b in before]
        + [raw()] * len(pieces),
        out_specs=(raw(),)
        + tuple(whole(o.shape) for o in out_shape[1:]),
        scratch_shapes=[
            pltpu.VMEM((2, width, 768), BF16),
            pltpu.VMEM((2, width, 768), BF16),
            pltpu.VMEM((n, width), BF16),
            pltpu.VMEM((n, width), F32),
            pltpu.VMEM((2, 8, 192, 768), BF16),
            pltpu.SemaphoreType.DMA((2, 2)),
            pltpu.SemaphoreType.DMA((2,)),
        ],
        compiler_params=PARAMS,
        cost_estimate=cost(12 * 10**10, 12 * 10**7, 2 * 10**6),
        name="hidden_b" if last else "hidden_a",
    )(where, x, norms, ct, *before, *pieces)


def mixer_kernel(n_pieces, where_ref, *refs):
    pieces, (mixer_ref, held) = refs[:n_pieces], refs[n_pieces:]
    for which, lead, rc, block, slot in blocks_in(pieces):
        ry, dp = block_at(where_ref, rc, block, slot)
        row = pl.multiple_of(dp * 96 + (where_ref[2] ^ (ry * 2 + rc)) * 24, 8)
        rows = pieces[which][lead].astype(F32)
        held[pl.ds(row, 24), 0:384] = rows[0:24]
        held[pl.ds(row, 24), 384:768] = rows[24:48]
    mixer_ref[...] = held[...].astype(BF16)


def place_mixer(where, pieces):
    return pl.pallas_call(
        functools.partial(mixer_kernel, len(pieces)),
        grid=(1,),
        out_shape=like(768, 768, dtype=BF16),
        in_specs=[scalars()]
        + [pl.BlockSpec((p.shape[0], 48, 384), lambda i: (0, 4, 0)) for p in pieces],
        out_specs=whole((768, 768)),
        scratch_shapes=[pltpu.VMEM((768, 768), F32)],
        compiler_params=PARAMS,
        cost_estimate=cost(10**6, 3 * 10**6, 0),
        name="place_mixer",
    )(where, *pieces)


def norms_kernel(n_pieces, *refs):
    left = jnp.zeros((8, 384), F32)
    right = jnp.zeros((8, 384), F32)
    for piece in refs[:n_pieces]:
        for lead in range(piece.shape[0]):
            rows = piece[lead].astype(F32)
            left = left + rows[0:8]
            right = right + rows[8:16]
    refs[n_pieces][...] = jnp.concatenate([left, right], axis=1)


def place_norms(pieces):
    return pl.pallas_call(
        functools.partial(norms_kernel, len(pieces)),
        grid=(1,),
        out_shape=like(8, 768),
        in_specs=[pl.BlockSpec((p.shape[0], 16, 384), lambda i: (0, 12, 0)) for p in pieces],
        out_specs=whole((8, 768)),
        compiler_params=PARAMS,
        cost_estimate=cost(10**5, 10**6, 0),
        name="place_norms",
    )(*pieces)


def finish_kernel(keep_ref, got_ref, qkv_ref, out_ref, *refs):
    total = keep_ref[...] + got_ref[...].astype(F32)
    qkv_ref[0] = total[0:96, :192]
    qkv_ref[1] = total[0:96, 192:]
    qkv_ref[2] = total[96:192, :192]
    out_ref[...] = jnp.transpose(total[96:192, 128:])[64:]
    if refs:
        refs[0][:, :384] = total[192:216]
        refs[0][:, 384:] = total[216:240]
        refs[1][:, :384] = total[240:248]
        refs[1][:, 384:] = total[248:256]


def finish(keep, got):
    shapes = [like(3, 96, 192), like(192, 96)]
    shapes += [like(24, 768), like(8, 768)] if keep.shape[0] > 192 else []
    return pl.pallas_call(
        finish_kernel,
        grid=(1,),
        out_shape=tuple(shapes),
        in_specs=[whole(keep.shape), whole(got.shape)],
        out_specs=tuple(whole(v.shape) for v in shapes),
        cost_estimate=cost(10**5, 10**6, 0),
        name="finish",
    )(keep, got)


class Order:
    def __init__(self, token):
        self.token = token

    def tie(self, *values):
        return values[0] if len(values) == 1 else values

    def go(self, value, route):
        return send(self.tie(value), route)


def after(arrived):
    return jnp.minimum(jnp.abs(arrived[(0,) * arrived.ndim].astype(F32)), 0.0)


def plus(a, b):
    return (a.astype(F32) + b.astype(F32)).astype(BF16)


class Gather:
    def __init__(self, order, shard):
        self.order, self.shard = order, shard

    def pairs(self):
        self.got = send(self.shard, SWAP_Z1)

    def second(self):
        self.pair = jnp.stack([self.shard, self.order.tie(self.got)])
        self.got = self.order.go(self.pair, SWAP_Z2)

    def sides(self, late=None):
        self.mine = jnp.concatenate([self.pair, self.order.tie(self.got)], axis=0)
        if late is not None:
            self.mine = self.mine + late.astype(BF16)
        self.got = self.order.go(self.mine, SIDE_ONE)

    def corners(self, late=None):
        self.eight = jnp.concatenate([self.mine, self.order.tie(self.got)], axis=0)
        if late is not None:
            self.eight = self.eight + late.astype(BF16)
        self.held, self.rest = [self.eight], [self.order.go(self.eight, SIDE_TWO)]

    def corner_one(self):
        self.held, self.rest = [self.mine], [self.order.go(self.mine, SIDE_TWO)]

    def corner_two(self):
        self.held.append(self.got)
        self.rest.append(self.order.go(self.got, SIDE_TWO))

    def cores(self, late=None):
        last = self.rest[-1] if late is None else self.rest[-1] + late.astype(BF16)
        every = self.held + self.rest[:-1] + [last]
        self.core = [self.order.go(v, SWAP_C) for v in every]

    def done(self):
        return self.held + self.rest + self.core


class Reduce:
    def __init__(self, order):
        self.order = order

    def cores(self, g_send):
        self.got = self.order.go(g_send, SWAP_C)

    def corners(self, g_keep, more=0.0, late=0.0, apart=False):
        got = self.order.tie(self.got)

        def joined(part):
            return (g_keep[part].astype(F32) + got[part].astype(F32) + more + late).astype(BF16)

        self.sent = joined(slice(8, 16))
        late = after(self.sent) if apart else 0.0
        self.keep = joined(slice(0, 8))
        self.got = self.order.go(self.sent, SIDE_TWO)

    def sides(self, late=0.0):
        got = self.order.tie(self.got)
        self.sent = (self.keep[4:].astype(F32) + got[4:].astype(F32) + late).astype(BF16)
        self.keep = plus(self.keep[:4], got[:4])
        self.got = self.order.go(self.sent, SIDE_ONE)

    def second(self, late=0.0):
        got = self.order.tie(self.got)
        self.sent = (self.keep[2:].astype(F32) + got[2:].astype(F32) + late).astype(BF16)
        self.keep = plus(self.keep[:2], got[:2])
        self.got = self.order.go(self.sent, SWAP_Z2)

    def pairs(self, late=0.0):
        got = self.order.tie(self.got)
        self.sent = (self.keep[1].astype(F32) + got[1].astype(F32) + late).astype(BF16)
        self.keep = self.keep[0].astype(F32) + got[0].astype(F32)
        self.got = self.order.go(self.sent, SWAP_Z1)

    def done(self):
        return self.keep, self.order.tie(self.got)


ROUTES = (SWAP_C, SWAP_Y, SWAP_YC)


def pack_attn(w_qkv, w_out):
    top = jnp.concatenate([w_qkv[0], w_qkv[1]], axis=1)
    low = jnp.concatenate([w_qkv[2], w_out.T], axis=1)
    return jnp.stack([top, low])


def unpack_attn(piece):
    grad_qkv = jnp.stack([piece[0, :, :192], piece[0, :, 192:], piece[1, :, :192]])
    return grad_qkv, piece[1, :, 192:].T


def full_gather(packed):
    return lax.all_gather(lax.all_gather(packed, "dp", axis=1, tiled=True), "tensor", axis=0)


def full_reduce(g_keep, g_send):
    rows, lanes = g_keep.shape[1:]
    full = jnp.stack([g_keep[:8], g_send[:8], g_keep[8:], g_send[8:]]).reshape(4, 8, 2, rows // 2, lanes)
    full = full.transpose(0, 2, 1, 3, 4).reshape(4, 2, 4 * rows, lanes).astype(F32)
    mine = lax.psum_scatter(full, "tensor", scatter_dimension=0, tiled=False)
    return lax.psum_scatter(mine, "dp", scatter_dimension=1, tiled=True)


def swap_all(pieces):
    got = lax.all_to_all(jnp.stack(pieces), "tensor", 0, 0, tiled=True)
    return [got[i] for i in range(4)]


def reorder(torus, groups, t):
    if not torus:
        return groups
    swap_c = (t & 1) == 1
    swap_y = (t >> 1) == 1
    groups = jnp.where(swap_c, jnp.stack([groups[1], groups[0], groups[3], groups[2]]), groups)
    return jnp.where(swap_y, jnp.stack([groups[2], groups[3], groups[0], groups[1]]), groups)


def padded(frames):
    return jnp.pad(frames, ((0, 0), (0, PAD - PATCHES), (0, 0))).reshape(2 * PAD, -1)


def trimmed(rows):
    return rows.reshape(2, PAD, -1)[:, :PATCHES]


def to_frames(torus, pieces, t):
    groups = reorder(torus, jnp.stack([p[:98].reshape(2, 49, -1) for p in pieces]), t)
    return groups.transpose(1, 0, 2, 3).reshape(2, PATCHES, -1)


def shards(
    torus,
    clip_tokens,
    time_qkv,
    time_out,
    time_mixer,
    space_qkv,
    space_out,
    hidden_in,
    hidden_out,
    norm_gain,
    norm_bias,
    cotangent,
):
    dp = lax.axis_index("dp")
    t = lax.axis_index("tensor")
    z, x = dp >> 1, dp & 1
    where = jnp.stack([z, x, t, t]).astype(jnp.int32)
    width = clip_tokens.shape[-1]
    tokens = clip_tokens[0].reshape(2, PATCHES, width)
    norm_rows = jnp.concatenate([norm_gain, norm_bias], axis=0)
    share = norm_rows.shape[1]
    order = Order(where)

    def by_patch_of(got):
        return jnp.stack(got).transpose(2, 0, 1, 3).reshape(392, width)

    time_w = pack_attn(time_qkv, time_out)
    groups = reorder(torus, tokens.reshape(2, 4, 49, width).transpose(1, 0, 2, 3), t)
    if torus:
        spread = lax.dynamic_update_slice(
            jnp.zeros((8, width), BF16), norm_rows, (0, (dp * 4 + t) * share)
        )
        timed = Gather(
            order,
            jnp.concatenate([time_w.reshape(192, 384), spread[:, :384], spread[:, 384:]], axis=0),
        )
        timed.pairs()
        moved = [order.go(groups[i + 1], ROUTES[i]) for i in range(3)]
        space_w = pack_attn(space_qkv, space_out)
        spaced = Gather(
            order,
            jnp.concatenate(
                [space_w.reshape(192, 384), time_mixer[:, :384], time_mixer[:, 384:]], axis=0
            ),
        )
        spaced.pairs()
        ff = Gather(order, jnp.concatenate([hidden_in, hidden_out.T], axis=0))
        ff.pairs()
        timed.second()
        spaced.second()
        by_patch = by_patch_of([groups[0]] + list(order.tie(*moved)))
        ff_first = after(ff.got)
        ff.second()
        base = order.tie(padded(tokens))
        ct = order.tie(padded(cotangent[0].reshape(2, PATCHES, width)))
        timed.sides(after(by_patch) + ff_first + after(base) + after(ct))
        timed.corners(after(spaced.got))
        spaced.sides()
        timed.cores()
        spaced.corners()
        ff.sides()
        time_p = timed.done()
        norms = place_norms(time_p)
    else:
        space_w = pack_attn(space_qkv, space_out)
        by_patch = by_patch_of(swap_all([groups[i] for i in range(4)]))
        ct = padded(cotangent[0].reshape(2, PATCHES, width))
        base = padded(tokens)
        time_p = [full_gather(time_w)]
        space_p = [full_gather(space_w)]
        ff_p = [full_gather(jnp.stack([hidden_in, hidden_out.T]))]
        mixer = lax.all_gather(time_mixer, AXES, axis=0, tiled=True)
        norms = lax.all_gather(norm_rows, AXES, axis=1, tiled=True).astype(F32)
        norms = jnp.pad(norms, ((0, 2), (0, 0)))

    def trade(pieces):
        if not torus:
            return swap_all(pieces)
        return [pieces[0]] + [order.go(pieces[i + 1], ROUTES[i]) for i in range(3)]

    by_patch = order.tie(by_patch)
    y_pieces, kept_time, high_time = time_fwd(
        torus, where, by_patch, norms, time_p, [ff.mine] if torus else []
    )
    y_pieces = trade(list(order.tie(*y_pieces)))
    if torus:
        spaced.cores()
        space_p = spaced.done()
        mixer = place_mixer(where, space_p)
    deps = []
    if torus:
        ff.corners(after(y_pieces[2]) + after(y_pieces[3]))
        deps = [ff.eight]
    x2, x1, mixer_in, kept_space, high_space = space_fwd(
        torus, where, base, norms, mixer, y_pieces, space_p, deps
    )
    if torus:
        ff.cores(after(x2))
        ff_p = ff.done()
    highs = jnp.stack([high_time[:, :3, 0], high_space[:, :3, 0]], axis=1)
    if torus:
        spots = reorder(torus, highs, t).reshape(1, 24)
        upper = lax.reduce_precision(spots, 8, 7)
        spots = jnp.concatenate([upper, spots - upper], axis=0)
        high_rows = lax.dynamic_update_slice(
            jnp.zeros((8, width), F32), spots, (6, (dp * 4 + t) * 24)
        )
    g1_ff, *before = hidden_both(torus, 0, where, x2, norms, ct, half(torus, ff_p, 1))
    if torus:
        red_ff, red_space, red_time = Reduce(order), Reduce(order), Reduce(order)
        red_ff.cores(g1_ff)
    g0_ff, out_rows, d_space, sums_three = hidden_both(
        torus, 1, where, x2, norms, ct, half(torus, ff_p, 0), tuple(before)
    )
    deps = []
    if torus:
        red_ff.corners(g0_ff)
        deps = [red_ff.sent]
    d_space = order.tie(d_space)
    g1_space, dh = attn_bwd(
        torus, True, 0, where, [d_space], x1, norms, kept_space, half(torus, space_p, 1), deps=deps
    )
    g1_space, dh = order.tie(g1_space, dh)
    if torus:
        red_space.cores(g1_space)
        deps = []
    dh = order.tie(dh)
    g0_space, sums_two, d_time, dmix, *dy = attn_bwd(
        torus,
        True,
        1,
        where,
        [d_space],
        x1,
        norms,
        kept_space,
        half(torus, space_p, 0),
        dh,
        (mixer_in, mixer),
        deps=deps,
    )
    g0_space, *dy = order.tie(g0_space, *dy)
    dy = trade(dy)
    if torus:
        red_ff.sides()
        deps = [red_ff.sent]
    dy = list(order.tie(*dy))
    g1_time, dh, dy, *passed = attn_bwd(
        torus,
        False,
        0,
        where,
        dy,
        by_patch,
        norms,
        kept_time,
        half(torus, time_p, 1),
        dmix=dmix,
        deps=deps,
        through=[g0_space] if torus else [],
    )
    g1_time, dh, dy = order.tie(g1_time, dh, dy)
    if torus:
        red_time.cores(g1_time)
        red_space.corners(passed[0])
        red_ff.second()
        deps = [red_ff.sent, red_space.sent]
    dh = order.tie(dh)
    g0_time, sums_one, *dx = attn_bwd(
        torus,
        False,
        1,
        where,
        [dy],
        by_patch,
        norms,
        kept_time,
        half(torus, time_p, 0),
        dh,
        dmix=dmix,
        deps=deps,
    )
    g0_time, sums_one, *dx = order.tie(g0_time, sums_one, *dx)

    sums = sums_one + (sums_two + sums_three)
    if torus:
        sums = sums + high_rows
        sums = sums + send(sums, SWAP_C)
        more = jnp.concatenate([sums[:, :384], sums[:, 384:]], axis=0)
        red_time.corners(
            g0_time, jnp.pad(more, ((240, 0), (0, 0))), after(red_space.got), apart=True
        )
        red_space.sides()
        red_space.second()
        dx = trade(dx)
        red_time.sides(after(red_space.sent))
        late = after(red_time.sent).astype(BF16)
        input_grad = trimmed(d_time) + to_frames(torus, [d + late for d in dx], t).astype(F32)
        red_time.second()
        red_space.pairs(after(red_time.sent))
        red_ff.pairs()
        space_qkv_grad, space_out_grad = finish(*red_space.done())
        ff_piece, got = red_ff.done()
        ff_piece = (ff_piece + got.astype(F32)).reshape(2, 96, 768)
        red_time.pairs()
        time_qkv_grad, time_out_grad, mixer_grad, total = finish(*red_time.done())
        mine = lax.dynamic_slice(total, (0, (dp * 4 + t) * share), (6, share))
        highest = jnp.max((total[6] + total[7]).reshape(32, 4, 2, 3), axis=0)
        highest = lax.dynamic_index_in_dim(highest, t, 0, keepdims=False)
    else:
        ff_piece = full_reduce(g0_ff, g1_ff)
        space_qkv_grad, space_out_grad = unpack_attn(full_reduce(g0_space, g1_space))
        time_qkv_grad, time_out_grad = unpack_attn(full_reduce(g0_time, g1_time))
        mixer_grad = lax.psum_scatter(dmix, AXES, scatter_dimension=0, tiled=True)
        input_grad = trimmed(d_time) + to_frames(torus, swap_all(dx), t).astype(F32)
        highest = lax.dynamic_index_in_dim(lax.pmax(highs, AXES), t, 0, keepdims=False)
        mine = lax.psum_scatter(sums[:6], AXES, scatter_dimension=1, tiled=True)
    qk_clip = jnp.sqrt(TAU / jnp.maximum(highest, TAU))
    return (
        trimmed(out_rows).reshape(1, 392, width),
        input_grad.reshape(1, 392, width),
        time_qkv_grad,
        time_out_grad,
        mixer_grad,
        space_qkv_grad,
        space_out_grad,
        ff_piece[0],
        ff_piece[1].T,
        mine[:3],
        mine[3:],
        qk_clip,
    )


def solution(mesh):
    sizes = dict(mesh.shape)
    torus = sizes["dp"] == 8 and sizes["tensor"] == 4
    in_specs = (
        P("dp", "tensor", None),
        P(None, "dp", "tensor"),
        P("tensor", "dp"),
        P(("dp", "tensor"), None),
        P(None, "dp", "tensor"),
        P("tensor", "dp"),
        P("dp", "tensor"),
        P("tensor", "dp"),
        P(None, ("dp", "tensor")),
        P(None, ("dp", "tensor")),
        P("dp", "tensor", None),
    )
    out_specs = (
        P("dp", "tensor", None),
        P("dp", "tensor", None),
        P(None, "dp", "tensor"),
        P("tensor", "dp"),
        P(("dp", "tensor"), None),
        P(None, "dp", "tensor"),
        P("tensor", "dp"),
        P("dp", "tensor"),
        P("tensor", "dp"),
        P(None, ("dp", "tensor")),
        P(None, ("dp", "tensor")),
        P(None, "tensor"),
    )
    body = functools.partial(shards, torus)
    return jax.shard_map(body, mesh=mesh, in_specs=in_specs, out_specs=out_specs, check_vma=False)
```

```python
import functools

import jax
import jax.numpy as jnp
from jax import lax
from jax.experimental import pallas as pl
from jax.experimental.pallas import tpu as pltpu
from jax.sharding import PartitionSpec as P

HD = 64
FRAMES = 8
PATCHES = 196
PAD = 208
SCALE = 0.125
TAU = 2.0
EPS = 1e-06
AXES = ("dp", "tensor")
F32 = jnp.float32
BF16 = jnp.bfloat16
PIECE = 112
VMEM_LIMIT = 60 * 1024 * 1024


def place(z, x, y, c):
    return ((z * 2 + x) * 2 + y) * 2 + c


ALL = [(z, x, y, c) for z in range(4) for x in range(2) for y in range(2) for c in range(2)]


def pairs(move, keep=lambda z, x, y, c: True):
    return [(place(*i), place(*move(*i))) for i in ALL if keep(*i)]


SWAP_C = pairs(lambda z, x, y, c: (z, x, y, 1 - c))
SWAP_Y = pairs(lambda z, x, y, c: (z, x, 1 - y, c))
SWAP_YC = pairs(lambda z, x, y, c: (z, x, 1 - y, 1 - c))
SWAP_X = pairs(lambda z, x, y, c: (z, 1 - x, y, c))
SWAP_Z1 = pairs(lambda z, x, y, c: (z ^ 1, x, y, c))
SWAP_Z2 = pairs(lambda z, x, y, c: (z ^ 2, x, y, c))
SIDE_ONE = pairs(lambda z, x, y, c: (z, x, 1 - y, c) if c else (z, 1 - x, y, c))
SIDE_TWO = pairs(lambda z, x, y, c: (z, 1 - x, y, c) if c else (z, x, 1 - y, c))


def send(value, route):
    return lax.ppermute(value, AXES, route)


def dot_nn(a, b):
    return lax.dot_general(a, b, (((1,), (0,)), ((), ())), preferred_element_type=F32)


def dot_nt(a, b):
    return lax.dot_general(a, b, (((1,), (1,)), ((), ())), preferred_element_type=F32)


def dot_tn(a, b):
    return lax.dot_general(a, b, (((0,), (0,)), ((), ())), preferred_element_type=F32)


def blocks_in(pieces):
    found, rc, block = [], 0, 0
    for which, piece in enumerate(pieces):
        for lead in range(piece.shape[0]):
            found.append((which, lead, rc, block, lead % 4))
            if lead % 4 == 3:
                block += 1
        if block == 4:
            rc, block = rc + 1, 0
    return found


def block_at(where_ref, rc, block, slot):
    low, high = block & 1, block >> 1
    first = ((where_ref[2] ^ rc) & 1) == 0
    rx = jnp.where(first, low, high)
    ry = jnp.where(first, high, low)
    return ry, (where_ref[0] ^ slot) * 2 + (where_ref[1] ^ rx)


def start_loads(torus, where_ref, pieces, stores, sems, groups):
    if not torus:
        for i, r in enumerate(groups):
            for b in range(2):
                pltpu.make_async_copy(pieces[0].at[r, b], stores[b].at[i], sems.at[i, b]).start()
        return
    every = len(groups) == 4
    for which, lead, rc, block, slot in blocks_in(pieces):
        ry, dp = block_at(where_ref, rc if every else groups[0], block, slot)
        i = ry * 2 + rc if every else ry
        row = pl.multiple_of(dp * 96, 96)
        for b in range(2):
            pltpu.make_async_copy(
                pieces[which].at[lead, pl.ds(b * 96, 96), :],
                stores[b].at[i, pl.ds(row, 96), :],
                sems.at[i, b],
            ).start()


def wait_loads(i, stores, sems):
    for b in range(2):
        pltpu.make_async_copy(stores[b].at[i], stores[b].at[i], sems.at[i, b]).wait()


def out_block(torus, where_ref, rc, step, dp):
    if not torus:
        return step * 8 + dp
    slot = where_ref[0] ^ (dp // 2)
    rx, ry = where_ref[1] ^ (dp % 2), step
    first = ((where_ref[2] ^ rc) & 1) == 0
    return jnp.where(first, ry, rx) * 8 + jnp.where(first, rx, ry) * 4 + slot


def peer(torus, where_ref, r):
    return where_ref[2] ^ r if torus else r


def put_grads(torus, where_ref, rc, step, stage, g_ref, sem, first, second, third=None):
    for dp in range(8):
        stage[step, dp, 0:96, :] = first[dp * 96 : (dp + 1) * 96]
        stage[step, dp, 96:192, :] = second[dp * 96 : (dp + 1) * 96]
        if third is not None:
            stage[step, dp, 192:, :] = third[dp]
        block = out_block(torus, where_ref, rc, step, dp)
        pltpu.make_async_copy(stage.at[step, dp], g_ref.at[block], sem.at[step]).start()


def wait_grads(stage, sem):
    for i in range(2):
        pltpu.make_async_copy(stage.at[i], stage.at[i], sem.at[i]).wait()


def normed(rows):
    mean = jnp.mean(rows, axis=-1, keepdims=True)
    centered = rows - mean
    inverse = lax.rsqrt(jnp.mean(centered * centered, axis=-1, keepdims=True) + EPS)
    return centered * inverse, inverse


def norm_low(scaled, norms_ref, norm):
    return (scaled * norms_ref[norm : norm + 1] + norms_ref[3 + norm : 4 + norm]).astype(BF16)


def norm_back(dh, scaled, inverse, gain):
    weighted = dh * gain
    return inverse * (
        weighted
        - jnp.mean(weighted, axis=-1, keepdims=True)
        - scaled * jnp.mean(weighted * scaled, axis=-1, keepdims=True)
    )


def norm_sums(dh, scaled, norm):
    gain = jnp.sum(dh * scaled, axis=0, keepdims=True)
    bias = jnp.sum(dh, axis=0, keepdims=True)
    row = lax.broadcasted_iota(jnp.int32, (8, dh.shape[1]), 0)
    return jnp.where(row == norm, gain, jnp.where(row == 3 + norm, bias, 0.0))


def ones_at(chosen):
    return jnp.where(chosen, 1.0, 0.0).astype(BF16)


def time_rows(r):
    row = lax.broadcasted_iota(jnp.int32, (PIECE, 392), 0)
    col = lax.broadcasted_iota(jnp.int32, (PIECE, 392), 1)
    return ones_at((((col >> 1) & 3) == r) & (row == (col & 1) * 49 + (col >> 3)))


def frame_rows(group):
    row = lax.broadcasted_iota(jnp.int32, (PIECE, 2 * PAD), 0)
    col = lax.broadcasted_iota(jnp.int32, (PIECE, 2 * PAD), 1)
    second = jnp.where(col >= PAD, 1, 0)
    patch = col - second * PAD - group * 49
    return ones_at((patch >= 0) & (patch < 49) & (row == second * 49 + patch))


def blocks_of(space):
    return ((0, PAD), (PAD, PAD)) if space else ((0, 192), (192, 200))


def keep_mask(space, size):
    row = lax.broadcasted_iota(jnp.int32, (size, size), 0)
    col = lax.broadcasted_iota(jnp.int32, (size, size), 1)
    if space:
        return row < PATCHES
    return (row >> 3) == (col >> 3)


def head_lanes(size):
    lane = lax.broadcasted_iota(jnp.int32, (size, 192), 1)
    return [(lane >= j * HD) & (lane < (j + 1) * HD) for j in range(3)]


def whole(shape):
    return pl.BlockSpec(shape, lambda i: (0,) * len(shape))


def raw():
    return pl.BlockSpec(memory_space=pl.ANY)


def scalars():
    return pl.BlockSpec(memory_space=pltpu.SMEM)


def like(*shape, dtype=F32):
    return jax.ShapeDtypeStruct(shape, dtype)


def cost(flops, size, exps):
    return pl.CostEstimate(flops=flops, bytes_accessed=size, transcendentals=exps)


PARAMS = pltpu.CompilerParams(vmem_limit_bytes=VMEM_LIMIT)


def heads_fwd(space, hidden, w_qk, w_vo, q_ref, k_ref, v_ref, o_ref, high_ref):
    qk = dot_nn(hidden, w_qk)
    q_ref[0] = qk[:, :192].astype(BF16)
    k_ref[0] = qk[:, 192:].astype(BF16)
    v_ref[0] = dot_nn(hidden, w_vo[:, :192]).astype(BF16)
    tops = [None, None, None]
    for start, size in blocks_of(space):
        q = q_ref[0, pl.ds(start, size), :]
        k = k_ref[0, pl.ds(start, size), :]
        v = v_ref[0, pl.ds(start, size), :]
        keep = keep_mask(space, size)
        zero = jnp.zeros_like(q)
        q = q * jnp.asarray(SCALE, BF16)
        mixed = None
        for j, mine in enumerate(head_lanes(size)):
            logits = jnp.where(keep, dot_nt(k, jnp.where(mine, q, zero)), -1e30)
            peak = jnp.max(logits, axis=0, keepdims=True)
            exponent = jnp.exp(logits - peak)
            weights = (exponent * (1.0 / jnp.sum(exponent, axis=0, keepdims=True))).astype(BF16)
            part = dot_tn(weights, jnp.where(mine, v, zero))
            mixed = part if mixed is None else mixed + part
            if space:
                col = lax.broadcasted_iota(jnp.int32, (1, size), 1)
                peak = jnp.where(col < PATCHES, peak, -1e30)
            top = jnp.max(peak, axis=1, keepdims=True)
            tops[j] = top if tops[j] is None else jnp.maximum(tops[j], top)
        o_ref[0, pl.ds(start, size), :] = mixed.astype(BF16)
    row8 = lax.broadcasted_iota(jnp.int32, (8, 128), 0)
    high = jnp.full((8, 128), -1e30, F32)
    for j in range(3):
        high = jnp.where(row8 == j, jnp.broadcast_to(tops[j], (8, 128)), high)
    high_ref[0] = high
    return dot_nt(o_ref[0], w_vo[:, 192:])


def time_fwd_kernel(torus, n_pieces, n_deps, where_ref, x_ref, norms_ref, *refs):
    pieces, refs = refs[:n_pieces], refs[n_pieces + n_deps :]
    outs, saved, refs = refs[:4], refs[4:9], refs[9:]
    w_qk, w_vo, h_ref, y_ref, sems = refs
    r = pl.program_id(0)

    @pl.when(r == 0)
    def _():
        start_loads(torus, where_ref, pieces, (w_qk, w_vo), sems, range(4))
        h_ref[...] = norm_low(normed(x_ref[...].astype(F32))[0], norms_ref, 0)
        y_ref[...] = jnp.zeros_like(y_ref)

    wait_loads(r, (w_qk, w_vo), sems)
    y_ref[...] += heads_fwd(False, h_ref[...], w_qk[r], w_vo[r], *saved)

    @pl.when(r == 3)
    def _():
        low = y_ref[...].astype(BF16)
        for i in range(4):
            outs[i][...] = dot_nn(time_rows(i), low).astype(BF16)


def space_fwd_kernel(torus, n_pieces, n_deps, where_ref, base_ref, norms_ref, mixer_ref, y0, y1, y2, y3, *refs):
    pieces, refs = refs[:n_pieces], refs[n_pieces + n_deps :]
    x2_ref, x1_ref, mixer_in_ref = refs[:3]
    saved, refs = refs[3:8], refs[8:]
    w_qk, w_vo, h_ref, sems = refs
    r = pl.program_id(0)

    @pl.when(r == 0)
    def _():
        start_loads(torus, where_ref, pieces, (w_qk, w_vo), sems, range(4))
        placed = None
        for i, piece in enumerate((y0, y1, y2, y3)):
            part = dot_tn(frame_rows(peer(torus, where_ref, i)), piece[...])
            placed = part if placed is None else placed + part
        mixer_in = placed.astype(BF16)
        mixer_in_ref[...] = mixer_in
        x1 = base_ref[...].astype(F32) + dot_nn(mixer_in, mixer_ref[...])
        x1_ref[...] = x1
        x2_ref[...] = x1
        h_ref[...] = norm_low(normed(x1)[0], norms_ref, 1)

    wait_loads(r, (w_qk, w_vo), sems)
    x2_ref[...] += heads_fwd(True, h_ref[...], w_qk[r], w_vo[r], *saved)


def per_group(shape, first=0, step=1):
    return pl.BlockSpec((1,) + shape, lambda i: (first + step * i,) + (0,) * len(shape))


def kept_shapes(n):
    return (like(4, n, 192, dtype=BF16),) * 4 + (like(4, 8, 128),)


def kept_specs(n):
    return (per_group((n, 192)),) * 4 + (per_group((8, 128)),)


def half(torus, pieces, rc):
    n = len(pieces) // 2
    return pieces[n * rc : n * rc + n] if torus else pieces


def attn_stores(groups, width):
    return [
        pltpu.VMEM((groups, width, 384), BF16),
        pltpu.VMEM((groups, width, 384), BF16),
    ]


def time_fwd(torus, where, x, norms, pieces, deps):
    n, width = x.shape
    outs = pl.pallas_call(
        functools.partial(time_fwd_kernel, torus, len(pieces), len(deps)),
        grid=(4,),
        out_shape=(like(PIECE, width, dtype=BF16),) * 4 + kept_shapes(n),
        in_specs=[scalars(), whole(x.shape), whole(norms.shape)]
        + [raw()] * (len(pieces) + len(deps)),
        out_specs=(whole((PIECE, width)),) * 4 + kept_specs(n),
        scratch_shapes=attn_stores(4, width)
        + [
            pltpu.VMEM((n, width), BF16),
            pltpu.VMEM((n, width), F32),
            pltpu.SemaphoreType.DMA((4, 2)),
        ],
        compiler_params=PARAMS,
        cost_estimate=cost(3 * 10**9, 12 * 10**6, 10**6),
        name="time_fwd",
    )(where, x, norms, *pieces, *deps)
    return list(outs[:4]), list(outs[4:8]), outs[8]


def space_fwd(torus, where, base, norms, mixer, y_pieces, pieces, deps):
    n, width = base.shape
    outs = pl.pallas_call(
        functools.partial(space_fwd_kernel, torus, len(pieces), len(deps)),
        grid=(4,),
        out_shape=(like(n, width), like(n, width), like(n, width, dtype=BF16)) + kept_shapes(n),
        in_specs=[scalars(), whole(base.shape), whole(norms.shape), whole(mixer.shape)]
        + [whole((PIECE, width))] * 4
        + [raw()] * (len(pieces) + len(deps)),
        out_specs=(whole((n, width)),) * 3 + kept_specs(n),
        scratch_shapes=attn_stores(4, width)
        + [pltpu.VMEM((n, width), BF16), pltpu.SemaphoreType.DMA((4, 2))],
        compiler_params=PARAMS,
        cost_estimate=cost(3 * 10**9, 12 * 10**6, 10**6),
        name="space_fwd",
    )(where, base, norms, mixer, *y_pieces, *pieces, *deps)
    return outs[0], outs[1], outs[2], list(outs[3:7]), outs[7]


def heads_bwd(space, dy, hidden, w_qk, w_vo, q_ref, k_ref, v_ref, o_ref, dq_ref, dk_ref, dv_ref):
    dv_ref[...] = dot_nn(dy, w_vo)[:, 192:].astype(BF16)
    for start, size in blocks_of(space):
        q = q_ref[0, pl.ds(start, size), :]
        k = k_ref[0, pl.ds(start, size), :]
        v = v_ref[0, pl.ds(start, size), :]
        do = dv_ref[pl.ds(start, size), :]
        keep = keep_mask(space, size)
        zero = jnp.zeros_like(q)
        q = q * jnp.asarray(SCALE, BF16)
        dq = dk = dv = None
        for mine in head_lanes(size):
            q_j = jnp.where(mine, q, zero)
            do_j = jnp.where(mine, do, zero)
            logits = jnp.where(keep, dot_nt(k, q_j), -1e30)
            exponent = jnp.exp(logits - jnp.max(logits, axis=0, keepdims=True))
            weights = exponent * (1.0 / jnp.sum(exponent, axis=0, keepdims=True))
            dweights = dot_nt(v, do_j)
            inner = jnp.sum(dweights * weights, axis=0, keepdims=True)
            dlogits = (weights * (dweights - inner)).astype(BF16)
            dv_j = dot_nn(weights.astype(BF16), do_j)
            dk_j = dot_nn(dlogits, q_j)
            dq_j = dot_tn(dlogits, jnp.where(mine, k, zero))
            dq = dq_j if dq is None else dq + dq_j
            dk = dk_j if dk is None else dk + dk_j
            dv = dv_j if dv is None else dv + dv_j
        dq_ref[pl.ds(start, size), :] = (dq * SCALE).astype(BF16)
        dk_ref[pl.ds(start, size), :] = dk.astype(BF16)
        dv_ref[pl.ds(start, size), :] = dv.astype(BF16)
    dqk = jnp.concatenate([dq_ref[...], dk_ref[...]], axis=1)
    dv = dv_ref[...]
    dh = dot_nt(dqk, w_qk) + dot_nt(dv, w_vo[:, :192])
    g_qk = dot_tn(hidden, dqk).astype(BF16)
    g_vo = jnp.concatenate([dot_tn(hidden, dv), dot_tn(dy, o_ref[0])], axis=1).astype(BF16)
    return dh, g_qk, g_vo


def bwd_kernel(torus, space, part, n_pieces, n_deps, n_through, where_ref, *refs):
    norm = 1 if space else 0
    last = part == 1
    n_dy = 1 if space or last else 4
    dy_in, refs = refs[:n_dy], refs[n_dy:]
    x_ref, norms_ref = refs[:2]
    kept, refs = refs[2:6], refs[6:]
    if last:
        dh_in, refs = refs[0], refs[1:]
    if space and last:
        mixer_in_ref, mixer_ref = refs[:2]
        refs = refs[2:]
    if not space:
        dmix_ref, refs = refs[0], refs[1:]
    pieces, refs = refs[:n_pieces], refs[n_pieces + n_deps + n_through :]
    g_ref, refs = refs[0], refs[1:]
    if not last:
        dh_out, refs = refs[0], refs[1:]
        if not space:
            dy_out, refs = refs[0], refs[1:]
    else:
        sums_ref, refs = refs[0], refs[1:]
        if space:
            d_ref, dmix_out = refs[:2]
            refs = refs[2:]
        outs, refs = refs[:4], refs[4:]
    w_qk, w_vo, h_ref, dy_ref, dq_ref, dk_ref, dv_ref, dh_ref, stage, sems, g_sem = refs[n_through:]
    step = pl.program_id(0)
    r = 2 * step + (1 - part)

    @pl.when(step == 0)
    def _():
        start_loads(torus, where_ref, pieces, (w_qk, w_vo), sems, (0, 2) if last else (1, 3))
        h_ref[...] = norm_low(normed(x_ref[...].astype(F32))[0], norms_ref, norm)
        if n_dy == 1:
            dy_ref[...] = dy_in[0][...].astype(BF16)
        else:
            placed = None
            for i in range(4):
                term = dot_tn(time_rows(i), dy_in[i][...])
                placed = term if placed is None else placed + term
            dy_ref[...] = placed.astype(BF16)
            dy_out[...] = placed.astype(BF16)
        dh_ref[...] = dh_in[...] if last else jnp.zeros_like(dh_ref)

    wait_loads(step, (w_qk, w_vo), sems)
    dh, g_qk, g_vo = heads_bwd(
        space, dy_ref[...], h_ref[...], w_qk[step], w_vo[step], *kept, dq_ref, dk_ref, dv_ref
    )
    dh_ref[...] += dh
    third = None
    if not space and torus:
        t = where_ref[2] ^ r
        third = []
        for dp in range(8):
            block = dmix_ref[pl.ds(pl.multiple_of(dp * 96 + t * 24, 8), 24), :]
            block = jnp.concatenate([block[:, :384], block[:, 384:], jnp.zeros((16, 384), F32)], axis=0)
            third.append(block.astype(BF16))
    put_grads(torus, where_ref, 1 - part, step, stage, g_ref, g_sem, g_qk, g_vo, third)

    @pl.when(step == 1)
    def _():
        if not last:
            dh_out[...] = dh_ref[...]
            wait_grads(stage, g_sem)
            return
        scaled, inverse = normed(x_ref[...].astype(F32))
        total = dh_ref[...]
        sums_ref[...] = norm_sums(total, scaled, norm)
        dx = norm_back(total, scaled, inverse, norms_ref[norm : norm + 1])
        if space:
            dx = dx + dy_in[0][...]
            d_ref[...] = dx
            low = dx.astype(BF16)
            dmix_out[...] = dot_tn(mixer_in_ref[...], low)
            low = dot_nt(low, mixer_ref[...]).astype(BF16)
            for i in range(4):
                outs[i][...] = dot_nn(frame_rows(peer(torus, where_ref, i)), low).astype(BF16)
        else:
            low = dx.astype(BF16)
            for i in range(4):
                outs[i][...] = dot_nn(time_rows(i), low).astype(BF16)
        wait_grads(stage, g_sem)


def attn_bwd(
    torus,
    space,
    part,
    where,
    dy,
    x,
    norms,
    kept,
    pieces,
    dh=None,
    mixing=(),
    dmix=None,
    deps=(),
    through=(),
):
    n, width = x.shape
    last = part == 1
    rows = 192 if space or not torus else 256
    small = like(PIECE, width, dtype=BF16)
    extra = ([] if dh is None else [dh]) + list(mixing) + ([] if dmix is None else [dmix])
    first = 1 + len(dy) + 2 + len(kept) + len(extra) + len(pieces) + len(deps)
    out_shape = [like(16, rows, 384, dtype=BF16)]
    if not last:
        out_shape += [like(n, width)] + ([] if space else [like(n, width, dtype=BF16)])
    else:
        out_shape += [like(8, width)]
        out_shape += [like(n, width), like(width, width)] if space else []
        out_shape += [small] * 4
    return pl.pallas_call(
        functools.partial(
            bwd_kernel, torus, space, part, len(pieces), len(deps), len(through)
        ),
        grid=(2,),
        out_shape=tuple(out_shape) + tuple(like(*v.shape, dtype=v.dtype) for v in through),
        in_specs=[scalars()]
        + [whole(d.shape) for d in dy]
        + [whole(x.shape), whole(norms.shape)]
        + [per_group((n, 192), 1 - part, 2)] * 4
        + [whole(e.shape) for e in extra]
        + [raw()] * (len(pieces) + len(deps) + len(through)),
        out_specs=(raw(),)
        + tuple(whole(o.shape) for o in out_shape[1:])
        + (raw(),) * len(through),
        input_output_aliases={first + i: len(out_shape) + i for i in range(len(through))},
        scratch_shapes=attn_stores(2, width)
        + [pltpu.VMEM((n, width), BF16)] * 2
        + [pltpu.VMEM((n, 192), BF16)] * 3
        + [
            pltpu.VMEM((n, width), F32),
            pltpu.VMEM((2, 8, rows, 384), BF16),
            pltpu.SemaphoreType.DMA((2, 2)),
            pltpu.SemaphoreType.DMA((2,)),
        ],
        compiler_params=PARAMS,
        cost_estimate=cost(10**8, 10**5, 0) if space and last else cost(8 * 10**10, 12 * 10**7, 10**6),
        name=("space" if space else "time") + ("_bwd_b" if last else "_bwd_a"),
    )(where, *dy, x, norms, *kept, *extra, *pieces, *deps, *through)


def hidden_kernel(torus, part, n_pieces, where_ref, x_ref, norms_ref, ct_ref, *refs):
    last = part == 1
    if last:
        out_in, dh_in = refs[:2]
        refs = refs[2:]
    pieces, refs = refs[:n_pieces], refs[n_pieces:]
    g_ref, out_ref, dx_ref = refs[:3]
    refs = refs[3:]
    if last:
        sums_ref, refs = refs[0], refs[1:]
    w_in, w_out, h_ref, dh_ref, stage, sems, g_sem = refs
    step = pl.program_id(0)

    @pl.when(step == 0)
    def _():
        start_loads(torus, where_ref, pieces, (w_in, w_out), sems, (0, 2) if last else (1, 3))
        x = x_ref[...]
        h_ref[...] = norm_low(normed(x)[0], norms_ref, 2)
        dh_ref[...] = dh_in[...] if last else jnp.zeros_like(dh_ref)
        out_ref[...] = out_in[...] if last else x

    wait_loads(step, (w_in, w_out), sems)
    hidden = h_ref[...]
    ct = ct_ref[...]
    up, down = w_in[step], w_out[step]
    pre = dot_nn(hidden, up)
    bell = 0.5 * (1.0 + lax.erf(pre * 0.7071067811865476))
    active = (pre * bell).astype(BF16)
    slope = bell + pre * (jnp.exp(-0.5 * pre * pre) * 0.3989422804014327)
    dpre = (dot_nn(ct, down) * slope).astype(BF16)
    out_ref[...] += dot_nt(active, down)
    dh_ref[...] += dot_nt(dpre, up)
    g_in = dot_tn(hidden, dpre).astype(BF16)
    g_out = dot_tn(ct, active).astype(BF16)
    put_grads(torus, where_ref, 1 - part, step, stage, g_ref, g_sem, g_in, g_out)

    @pl.when(step == 1)
    def _():
        dh = dh_ref[...]
        if not last:
            dx_ref[...] = dh
            wait_grads(stage, g_sem)
            return
        scaled, inverse = normed(x_ref[...])
        dx_ref[...] = ct_ref[...].astype(F32) + norm_back(dh, scaled, inverse, norms_ref[2:3])
        sums_ref[...] = norm_sums(dh, scaled, 2)
        wait_grads(stage, g_sem)


def hidden_both(torus, part, where, x, norms, ct, pieces, before=()):
    n, width = x.shape
    last = part == 1
    out_shape = [like(16, 192, 768, dtype=BF16), like(n, width), like(n, width)]
    out_shape += [like(8, width)] if last else []
    return pl.pallas_call(
        functools.partial(hidden_kernel, torus, part, len(pieces)),
        grid=(2,),
        out_shape=tuple(out_shape),
        in_specs=[scalars(), whole(x.shape), whole(norms.shape), whole(ct.shape)]
        + [whole(b.shape) for b in before]
        + [raw()] * len(pieces),
        out_specs=(raw(),)
        + tuple(whole(o.shape) for o in out_shape[1:]),
        scratch_shapes=[
            pltpu.VMEM((2, width, 768), BF16),
            pltpu.VMEM((2, width, 768), BF16),
            pltpu.VMEM((n, width), BF16),
            pltpu.VMEM((n, width), F32),
            pltpu.VMEM((2, 8, 192, 768), BF16),
            pltpu.SemaphoreType.DMA((2, 2)),
            pltpu.SemaphoreType.DMA((2,)),
        ],
        compiler_params=PARAMS,
        cost_estimate=cost(12 * 10**10, 12 * 10**7, 2 * 10**6),
        name="hidden_b" if last else "hidden_a",
    )(where, x, norms, ct, *before, *pieces)


def mixer_kernel(n_pieces, where_ref, *refs):
    pieces, (mixer_ref, held) = refs[:n_pieces], refs[n_pieces:]
    for which, lead, rc, block, slot in blocks_in(pieces):
        ry, dp = block_at(where_ref, rc, block, slot)
        row = pl.multiple_of(dp * 96 + (where_ref[2] ^ (ry * 2 + rc)) * 24, 8)
        rows = pieces[which][lead].astype(F32)
        held[pl.ds(row, 24), 0:384] = rows[0:24]
        held[pl.ds(row, 24), 384:768] = rows[24:48]
    mixer_ref[...] = held[...].astype(BF16)


def place_mixer(where, pieces):
    return pl.pallas_call(
        functools.partial(mixer_kernel, len(pieces)),
        grid=(1,),
        out_shape=like(768, 768, dtype=BF16),
        in_specs=[scalars()]
        + [pl.BlockSpec((p.shape[0], 48, 384), lambda i: (0, 4, 0)) for p in pieces],
        out_specs=whole((768, 768)),
        scratch_shapes=[pltpu.VMEM((768, 768), F32)],
        compiler_params=PARAMS,
        cost_estimate=cost(10**6, 3 * 10**6, 0),
        name="place_mixer",
    )(where, *pieces)


def norms_kernel(n_pieces, *refs):
    left = jnp.zeros((8, 384), F32)
    right = jnp.zeros((8, 384), F32)
    for piece in refs[:n_pieces]:
        for lead in range(piece.shape[0]):
            rows = piece[lead].astype(F32)
            left = left + rows[0:8]
            right = right + rows[8:16]
    refs[n_pieces][...] = jnp.concatenate([left, right], axis=1)


def place_norms(pieces):
    return pl.pallas_call(
        functools.partial(norms_kernel, len(pieces)),
        grid=(1,),
        out_shape=like(8, 768),
        in_specs=[pl.BlockSpec((p.shape[0], 16, 384), lambda i: (0, 12, 0)) for p in pieces],
        out_specs=whole((8, 768)),
        compiler_params=PARAMS,
        cost_estimate=cost(10**5, 10**6, 0),
        name="place_norms",
    )(*pieces)


def pack_kernel(where_ref, qkv_ref, out_ref, gain_ref, bias_ref, shard_ref):
    shard_ref[0:96, 0:192] = qkv_ref[0]
    shard_ref[0:96, 192:384] = qkv_ref[1]
    shard_ref[96:192, 0:192] = qkv_ref[2]
    shard_ref[96:192, 192:384] = jnp.transpose(out_ref[...].astype(F32)).astype(BF16)
    first = (where_ref[0] * 8 + where_ref[1] * 4 + where_ref[2]) * 24
    row = lax.broadcasted_iota(jnp.int32, (24, 768), 0)
    col = lax.broadcasted_iota(jnp.int32, (24, 768), 1)
    spot = ones_at(col == first + row)
    rows = jnp.concatenate(
        [dot_nn(gain_ref[...], spot), dot_nn(bias_ref[...], spot), jnp.zeros((2, 768), F32)], axis=0
    ).astype(BF16)
    shard_ref[192:200, :] = rows[:, :384]
    shard_ref[200:208, :] = rows[:, 384:]


def pack_time(where, w_qkv, w_out, gain, bias):
    return pl.pallas_call(
        pack_kernel,
        grid=(1,),
        out_shape=like(208, 384, dtype=BF16),
        in_specs=[scalars()] + [whole(v.shape) for v in (w_qkv, w_out, gain, bias)],
        out_specs=whole((208, 384)),
        cost_estimate=cost(10**5, 10**5, 0),
        name="pack_time",
    )(where, w_qkv, w_out, gain, bias)


def finish_kernel(keep_ref, got_ref, qkv_ref, out_ref, *refs):
    total = keep_ref[...] + got_ref[...].astype(F32)
    qkv_ref[0] = total[0:96, :192]
    qkv_ref[1] = total[0:96, 192:]
    qkv_ref[2] = total[96:192, :192]
    out_ref[...] = jnp.transpose(total[96:192, 128:])[64:]
    if refs:
        refs[0][:, :384] = total[192:216]
        refs[0][:, 384:] = total[216:240]
        refs[1][:, :384] = total[240:248]
        refs[1][:, 384:] = total[248:256]


def finish(keep, got):
    shapes = [like(3, 96, 192), like(192, 96)]
    shapes += [like(24, 768), like(8, 768)] if keep.shape[0] > 192 else []
    return pl.pallas_call(
        finish_kernel,
        grid=(1,),
        out_shape=tuple(shapes),
        in_specs=[whole(keep.shape), whole(got.shape)],
        out_specs=tuple(whole(v.shape) for v in shapes),
        cost_estimate=cost(10**5, 10**6, 0),
        name="finish",
    )(keep, got)


class Order:
    def __init__(self, token):
        self.token = token

    def tie(self, *values):
        return values[0] if len(values) == 1 else values

    def go(self, value, route):
        return send(self.tie(value), route)


def after(arrived):
    return jnp.minimum(jnp.abs(arrived[(0,) * arrived.ndim].astype(F32)), 0.0)


def plus(a, b):
    return (a.astype(F32) + b.astype(F32)).astype(BF16)


class Gather:
    def __init__(self, order, shard):
        self.order, self.shard = order, shard

    def pairs(self):
        self.got = send(self.shard, SWAP_Z1)

    def second(self):
        self.pair = jnp.stack([self.shard, self.order.tie(self.got)])
        self.got = self.order.go(self.pair, SWAP_Z2)

    def sides(self, late=None):
        self.mine = jnp.concatenate([self.pair, self.order.tie(self.got)], axis=0)
        if late is not None:
            self.mine = self.mine + late.astype(BF16)
        self.got = self.order.go(self.mine, SIDE_ONE)

    def corners(self, late=None):
        self.eight = jnp.concatenate([self.mine, self.order.tie(self.got)], axis=0)
        if late is not None:
            self.eight = self.eight + late.astype(BF16)
        self.held, self.rest = [self.eight], [self.order.go(self.eight, SIDE_TWO)]

    def corner_one(self):
        self.held, self.rest = [self.mine], [self.order.go(self.mine, SIDE_TWO)]

    def corner_two(self):
        self.held.append(self.got)
        self.rest.append(self.order.go(self.got, SIDE_TWO))

    def cores(self, late=None):
        last = self.rest[-1] if late is None else self.rest[-1] + late.astype(BF16)
        every = self.held + self.rest[:-1] + [last]
        self.core = [self.order.go(v, SWAP_C) for v in every]

    def done(self):
        return self.held + self.rest + self.core


class Reduce:
    def __init__(self, order):
        self.order = order

    def cores(self, g_send):
        self.got = self.order.go(g_send, SWAP_C)

    def corners(self, g_keep, more=0.0, late=0.0, apart=False):
        got = self.order.tie(self.got)

        def joined(part):
            return (g_keep[part].astype(F32) + got[part].astype(F32) + more + late).astype(BF16)

        self.sent = joined(slice(8, 16))
        late = after(self.sent) if apart else 0.0
        self.keep = joined(slice(0, 8))
        self.got = self.order.go(self.sent, SIDE_TWO)

    def sides(self, late=0.0):
        got = self.order.tie(self.got)
        self.sent = (self.keep[4:].astype(F32) + got[4:].astype(F32) + late).astype(BF16)
        self.keep = plus(self.keep[:4], got[:4])
        self.got = self.order.go(self.sent, SIDE_ONE)

    def second(self, late=0.0):
        got = self.order.tie(self.got)
        self.sent = (self.keep[2:].astype(F32) + got[2:].astype(F32) + late).astype(BF16)
        self.keep = plus(self.keep[:2], got[:2])
        self.got = self.order.go(self.sent, SWAP_Z2)

    def pairs(self, late=0.0):
        got = self.order.tie(self.got)
        self.sent = (self.keep[1].astype(F32) + got[1].astype(F32) + late).astype(BF16)
        self.keep = self.keep[0].astype(F32) + got[0].astype(F32)
        self.got = self.order.go(self.sent, SWAP_Z1)

    def done(self):
        return self.keep, self.order.tie(self.got)


ROUTES = (SWAP_C, SWAP_Y, SWAP_YC)


def pack_attn(w_qkv, w_out):
    top = jnp.concatenate([w_qkv[0], w_qkv[1]], axis=1)
    low = jnp.concatenate([w_qkv[2], w_out.T], axis=1)
    return jnp.stack([top, low])


def unpack_attn(piece):
    grad_qkv = jnp.stack([piece[0, :, :192], piece[0, :, 192:], piece[1, :, :192]])
    return grad_qkv, piece[1, :, 192:].T


def full_gather(packed):
    return lax.all_gather(lax.all_gather(packed, "dp", axis=1, tiled=True), "tensor", axis=0)


def full_reduce(g_keep, g_send):
    rows, lanes = g_keep.shape[1:]
    full = jnp.stack([g_keep[:8], g_send[:8], g_keep[8:], g_send[8:]]).reshape(4, 8, 2, rows // 2, lanes)
    full = full.transpose(0, 2, 1, 3, 4).reshape(4, 2, 4 * rows, lanes).astype(F32)
    mine = lax.psum_scatter(full, "tensor", scatter_dimension=0, tiled=False)
    return lax.psum_scatter(mine, "dp", scatter_dimension=1, tiled=True)


def swap_all(pieces):
    got = lax.all_to_all(jnp.stack(pieces), "tensor", 0, 0, tiled=True)
    return [got[i] for i in range(4)]


def reorder(torus, groups, t):
    if not torus:
        return groups
    swap_c = (t & 1) == 1
    swap_y = (t >> 1) == 1
    groups = jnp.where(swap_c, jnp.stack([groups[1], groups[0], groups[3], groups[2]]), groups)
    return jnp.where(swap_y, jnp.stack([groups[2], groups[3], groups[0], groups[1]]), groups)


def padded(frames):
    return jnp.pad(frames, ((0, 0), (0, PAD - PATCHES), (0, 0))).reshape(2 * PAD, -1)


def trimmed(rows):
    return rows.reshape(2, PAD, -1)[:, :PATCHES]


def to_frames(torus, pieces, t):
    groups = reorder(torus, jnp.stack([p[:98].reshape(2, 49, -1) for p in pieces]), t)
    return groups.transpose(1, 0, 2, 3).reshape(2, PATCHES, -1)


def shards(
    torus,
    clip_tokens,
    time_qkv,
    time_out,
    time_mixer,
    space_qkv,
    space_out,
    hidden_in,
    hidden_out,
    norm_gain,
    norm_bias,
    cotangent,
):
    dp = lax.axis_index("dp")
    t = lax.axis_index("tensor")
    z, x = dp >> 1, dp & 1
    where = jnp.stack([z, x, t, t]).astype(jnp.int32)
    width = clip_tokens.shape[-1]
    tokens = clip_tokens[0].reshape(2, PATCHES, width)
    norm_rows = jnp.concatenate([norm_gain, norm_bias], axis=0)
    share = norm_rows.shape[1]
    order = Order(where)

    def by_patch_of(got):
        return jnp.stack(got).transpose(2, 0, 1, 3).reshape(392, width)

    time_w = pack_attn(time_qkv, time_out)
    groups = reorder(torus, tokens.reshape(2, 4, 49, width).transpose(1, 0, 2, 3), t)
    if torus:
        timed = Gather(order, pack_time(where, time_qkv, time_out, norm_gain, norm_bias))
        timed.pairs()
        moved = [order.go(groups[i + 1], ROUTES[i]) for i in range(3)]
        space_w = pack_attn(space_qkv, space_out)
        spaced = Gather(
            order,
            jnp.concatenate(
                [space_w.reshape(192, 384), time_mixer[:, :384], time_mixer[:, 384:]], axis=0
            ),
        )
        spaced.pairs()
        ff = Gather(order, jnp.concatenate([hidden_in, hidden_out.T], axis=0))
        ff.pairs()
        timed.second()
        spaced.second()
        by_patch = by_patch_of([groups[0]] + list(order.tie(*moved)))
        ff_first = after(ff.got)
        ff.second()
        base = order.tie(padded(tokens))
        ct = order.tie(padded(cotangent[0].reshape(2, PATCHES, width)))
        timed.sides(after(by_patch) + ff_first + after(base) + after(ct))
        timed.corners(after(spaced.got))
        spaced.sides()
        timed.cores()
        spaced.corners()
        ff.sides()
        time_p = timed.done()
        norms = place_norms(time_p)
    else:
        space_w = pack_attn(space_qkv, space_out)
        by_patch = by_patch_of(swap_all([groups[i] for i in range(4)]))
        ct = padded(cotangent[0].reshape(2, PATCHES, width))
        base = padded(tokens)
        time_p = [full_gather(time_w)]
        space_p = [full_gather(space_w)]
        ff_p = [full_gather(jnp.stack([hidden_in, hidden_out.T]))]
        mixer = lax.all_gather(time_mixer, AXES, axis=0, tiled=True)
        norms = lax.all_gather(norm_rows, AXES, axis=1, tiled=True).astype(F32)
        norms = jnp.pad(norms, ((0, 2), (0, 0)))

    def trade(pieces):
        if not torus:
            return swap_all(pieces)
        return [pieces[0]] + [order.go(pieces[i + 1], ROUTES[i]) for i in range(3)]

    by_patch = order.tie(by_patch)
    y_pieces, kept_time, high_time = time_fwd(
        torus, where, by_patch, norms, time_p, [ff.mine] if torus else []
    )
    y_pieces = trade(list(order.tie(*y_pieces)))
    if torus:
        spaced.cores()
        space_p = spaced.done()
        mixer = place_mixer(where, space_p)
    deps = []
    if torus:
        ff.corners(after(y_pieces[2]) + after(y_pieces[3]))
        deps = [ff.eight]
    x2, x1, mixer_in, kept_space, high_space = space_fwd(
        torus, where, base, norms, mixer, y_pieces, space_p, deps
    )
    if torus:
        ff.cores(after(x2))
        ff_p = ff.done()
    highs = jnp.stack([high_time[:, :3, 0], high_space[:, :3, 0]], axis=1)
    if torus:
        spots = reorder(torus, highs, t).reshape(1, 24)
        upper = lax.reduce_precision(spots, 8, 7)
        spots = jnp.concatenate([upper, spots - upper], axis=0)
        high_rows = lax.dynamic_update_slice(
            jnp.zeros((8, width), F32), spots, (6, (dp * 4 + t) * 24)
        )
    g1_ff, *before = hidden_both(torus, 0, where, x2, norms, ct, half(torus, ff_p, 1))
    if torus:
        red_ff, red_space, red_time = Reduce(order), Reduce(order), Reduce(order)
        red_ff.cores(g1_ff)
    g0_ff, out_rows, d_space, sums_three = hidden_both(
        torus, 1, where, x2, norms, ct, half(torus, ff_p, 0), tuple(before)
    )
    deps = []
    if torus:
        red_ff.corners(g0_ff)
        deps = [red_ff.sent]
    d_space = order.tie(d_space)
    g1_space, dh = attn_bwd(
        torus, True, 0, where, [d_space], x1, norms, kept_space, half(torus, space_p, 1), deps=deps
    )
    g1_space, dh = order.tie(g1_space, dh)
    if torus:
        red_space.cores(g1_space)
        deps = []
    dh = order.tie(dh)
    g0_space, sums_two, d_time, dmix, *dy = attn_bwd(
        torus,
        True,
        1,
        where,
        [d_space],
        x1,
        norms,
        kept_space,
        half(torus, space_p, 0),
        dh,
        (mixer_in, mixer),
        deps=deps,
    )
    g0_space, *dy = order.tie(g0_space, *dy)
    dy = trade(dy)
    if torus:
        red_ff.sides()
        deps = [red_ff.sent]
    dy = list(order.tie(*dy))
    g1_time, dh, dy, *passed = attn_bwd(
        torus,
        False,
        0,
        where,
        dy,
        by_patch,
        norms,
        kept_time,
        half(torus, time_p, 1),
        dmix=dmix,
        deps=deps,
        through=[g0_space] if torus else [],
    )
    g1_time, dh, dy = order.tie(g1_time, dh, dy)
    if torus:
        red_time.cores(g1_time)
        red_space.corners(passed[0])
        red_ff.second()
        deps = [red_ff.sent, red_space.sent]
    dh = order.tie(dh)
    g0_time, sums_one, *dx = attn_bwd(
        torus,
        False,
        1,
        where,
        [dy],
        by_patch,
        norms,
        kept_time,
        half(torus, time_p, 0),
        dh,
        dmix=dmix,
        deps=deps,
    )
    g0_time, sums_one, *dx = order.tie(g0_time, sums_one, *dx)

    sums = sums_one + (sums_two + sums_three)
    if torus:
        sums = sums + high_rows
        sums = sums + send(sums, SWAP_C)
        more = jnp.concatenate([sums[:, :384], sums[:, 384:]], axis=0)
        red_time.corners(
            g0_time, jnp.pad(more, ((240, 0), (0, 0))), apart=True
        )
        red_space.sides()
        red_space.second()
        dx = trade(dx)
        red_time.sides()
        late = after(red_time.sent).astype(BF16)
        input_grad = trimmed(d_time) + to_frames(torus, [d + late for d in dx], t).astype(F32)
        red_time.second()
        red_space.pairs(after(red_time.sent))
        red_ff.pairs()
        space_qkv_grad, space_out_grad = finish(*red_space.done())
        ff_piece, got = red_ff.done()
        ff_piece = (ff_piece + got.astype(F32)).reshape(2, 96, 768)
        red_time.pairs()
        time_qkv_grad, time_out_grad, mixer_grad, total = finish(*red_time.done())
        mine = lax.dynamic_slice(total, (0, (dp * 4 + t) * share), (6, share))
        highest = jnp.max((total[6] + total[7]).reshape(32, 4, 2, 3), axis=0)
        highest = lax.dynamic_index_in_dim(highest, t, 0, keepdims=False)
    else:
        ff_piece = full_reduce(g0_ff, g1_ff)
        space_qkv_grad, space_out_grad = unpack_attn(full_reduce(g0_space, g1_space))
        time_qkv_grad, time_out_grad = unpack_attn(full_reduce(g0_time, g1_time))
        mixer_grad = lax.psum_scatter(dmix, AXES, scatter_dimension=0, tiled=True)
        input_grad = trimmed(d_time) + to_frames(torus, swap_all(dx), t).astype(F32)
        highest = lax.dynamic_index_in_dim(lax.pmax(highs, AXES), t, 0, keepdims=False)
        mine = lax.psum_scatter(sums[:6], AXES, scatter_dimension=1, tiled=True)
    qk_clip = jnp.sqrt(TAU / jnp.maximum(highest, TAU))
    return (
        trimmed(out_rows).reshape(1, 392, width),
        input_grad.reshape(1, 392, width),
        time_qkv_grad,
        time_out_grad,
        mixer_grad,
        space_qkv_grad,
        space_out_grad,
        ff_piece[0],
        ff_piece[1].T,
        mine[:3],
        mine[3:],
        qk_clip,
    )


def solution(mesh):
    sizes = dict(mesh.shape)
    torus = sizes["dp"] == 8 and sizes["tensor"] == 4
    in_specs = (
        P("dp", "tensor", None),
        P(None, "dp", "tensor"),
        P("tensor", "dp"),
        P(("dp", "tensor"), None),
        P(None, "dp", "tensor"),
        P("tensor", "dp"),
        P("dp", "tensor"),
        P("tensor", "dp"),
        P(None, ("dp", "tensor")),
        P(None, ("dp", "tensor")),
        P("dp", "tensor", None),
    )
    out_specs = (
        P("dp", "tensor", None),
        P("dp", "tensor", None),
        P(None, "dp", "tensor"),
        P("tensor", "dp"),
        P(("dp", "tensor"), None),
        P(None, "dp", "tensor"),
        P("tensor", "dp"),
        P("dp", "tensor"),
        P("tensor", "dp"),
        P(None, ("dp", "tensor")),
        P(None, ("dp", "tensor")),
        P(None, "tensor"),
    )
    body = functools.partial(shards, torus)
    return jax.shard_map(body, mesh=mesh, in_specs=in_specs, out_specs=out_specs, check_vma=False)
```
